512 devices in a mesh: tile: 32 (over x, z), row: 16 (over y, core).
Axes of the slice: x: 4, y: 8, z: 8, core: 2. Of those that a mesh axis runs over, the one named last changes fastest.
Arguments:
- voltage: float32 [32, 16, 1, 64, 128], P('tile', 'row'), may hold values from -6 to 6
- history: bfloat16 [32, 16, 32, 64, 128], P('tile', 'row'), may hold values from -6 to 6
- far_blocks: bfloat16 [32, 16, 32, 128, 128], P('tile', 'row'), may hold values from -0.09375 to 0.09375
- far_target: int32 [32, 16, 32, 1], P('tile', 'row'), may hold values from 0 to 31; in each aligned block of 32 rows (0 to 31, 32 to 63, ..., all dimensions but the last counted through in order) at most 2 rows name the same one
- far_delay: int32 [32, 16, 32], P('tile', 'row'), may hold values from 1 to 32
- near_blocks: bfloat16 [32, 16, 3, 128, 128], P('tile', 'row'), may hold values from -0.15625 to 0.15625
- near_link: int32 [32, 16, 2], P('tile', 'row'), may hold values 0 or 1
- jacobi_blocks: bfloat16 [32, 16, 128, 128], P('tile', 'row'), may hold values from -0.21875 to 0.21875
Outputs:
- currents: float32 [32, 16, 1, 64, 128], P('tile', 'row')
The draws below stay inside these ranges and needn't reach their ends.
Inputs may be any that keep to these rules, and one draw needn't show every extreme that they name: `far_target`: among the 32 entries of one tile at most 2 name the same target, and some tile has exactly 2 naming one target.
All inputs are finite; a program needn't handle non-finite values. No bound on the sum of `near_link` on one device may be relied on, other than what follows from the above.
Results may differ from the reference program's by a relative error of at most 0.0003.
Values sent between devices are 32-bit elements; how exact they have to be, the bound alone decides.
No kernel may reach another device: no remote copies, remote signals or barrier semaphores. Data moves between devices by JAX's collectives and lax.ppermute only.
A program may use at most 64 MiB of HBM per device.

```python
import math
import jax
import jax.numpy as jnp
import numpy as np
from jax import lax

SEG = 128
COLS = 64
K = 32
L = 32
ITERS = 5
STEPS = 1
TA = 32
TB = 16
CAP = 2


def touch_ends(values, own_key, low, largest):
    longest = values.shape.index(max(values.shape))
    spots = []
    for shift in (0, 1):
        where = [jax.random.randint(jax.random.fold_in(own_key, axis), (), 0, length) for axis, length in enumerate(values.shape)]
        where[longest] = (where[longest] + shift) % values.shape[longest]
        spots.append(tuple(where))
    return values.at[spots[0]].set(low).at[spots[1]].set(largest)


def block_levels(stream_key, extent, cuts, smallest, top_value):
    loudness = 1.0
    for position, parts in cuts:
        heights = jax.random.uniform(jax.random.fold_in(jax.random.fold_in(stream_key, 6), position), (parts,), jnp.float32, smallest / len(cuts), top_value / len(cuts))
        loudness = loudness * jnp.repeat(jnp.exp(heights), extent[position] // parts).reshape((-1,) + (1,) * (len(extent) - 1 - position))
    return loudness


def routed_block(key, own, number, rows, count, top, most, skew):
    sequence = jax.random.permutation(key, count)
    crowded, ordinary = load_shares(count, rows * top, most, skew, True), load_shares(count, rows * top, most, skew, False)
    places = jnp.arange(count)

    def named(sizes, turn):
        used = int((sizes > 0).sum())
        fixed = max(1, used // 4)
        moved = fixed + (places - fixed + turn * (used - fixed)) % max(1, count - fixed)
        return jnp.zeros((count,), jnp.int32).at[sequence[jnp.where(places < fixed, places, moved)]].set(jnp.asarray(sizes, jnp.int32))

    sizes = jnp.where(number % 4 == 0, named(crowded, number // 4), named(ordinary, number - number // 4 - 1))
    mixed = jax.random.permutation(jax.random.fold_in(own, 3), count)
    donor, sink = mixed[0:count // 2 * 2:2], mixed[1:count // 2 * 2:2]
    slack = jnp.minimum(sizes[donor] - 1, most - sizes[sink]) // 2
    slack = jnp.where((donor == sequence[0]) | (sink == sequence[0]) | (sizes[sink] == 0), 0, jnp.maximum(slack, 0))
    moved = jax.random.randint(jax.random.fold_in(own, 4), (count // 2,), 0, 1 << 20) % (slack + 1)
    sizes = sizes.at[donor].add(-moved).at[sink].add(moved)
    items = jnp.searchsorted(jnp.cumsum(sizes), jnp.arange(rows * top), side="right").astype(jnp.int32)
    grid = items.reshape(top, rows).T
    grid = grid[jax.random.permutation(jax.random.fold_in(own, 1), rows)]
    turn = jax.random.randint(jax.random.fold_in(own, 2), (rows, 1), 0, top)
    return jnp.take_along_axis(grid, (jnp.arange(top)[None, :] + turn) % top, axis=1)


def load_shares(number_of, total, bound, skew, full):
    weights = [(1 << 20) // math.isqrt(rank ** skew) + 1 for rank in range(1, number_of + 1)]
    largest = bound if full else min(bound, max(-(-total // number_of), total * weights[0] // sum(weights)))
    least = 1 if total - largest >= number_of - 1 else 0
    holding, surplus = [largest] + [least] * (number_of - 1), total - largest - least * (number_of - 1)
    while surplus > 0:
        movable = [i for i in range(1, number_of) if holding[i] < largest] or [i for i in range(1, number_of) if holding[i] < bound]
        pool, left = sum([weights[i] for i in movable]), surplus
        for i in movable:
            more = min(bound - holding[i], max(1, left * weights[i] // pool), surplus)
            holding[i] = holding[i] + more
            surplus = surplus - more
    return np.array(holding)


def centred(key, extent, width, limit, shards=(), held_as=jnp.bfloat16):
    array = width * jax.random.normal(key, extent, jnp.float32)
    if shards:
        array = array * block_levels(key, extent, shards, -0.22, 0.18)
    return jnp.clip(array, -limit, limit).astype(held_as)


def setup_inputs(seed: int = 0) -> dict:
    key_list = jax.random.split(jax.random.key(seed), 9)
    voltage = centred(key_list[0], (TA, TB, STEPS, COLS, SEG), 1.0, 6.0, ((0, 32), (1, 16)), jnp.float32)
    history = centred(key_list[1], (TA, TB, K, COLS, SEG), 1.0, 6.0, ((0, 32), (1, 16)))
    far_blocks = centred(key_list[2], (TA, TB, L, SEG, SEG), (SEG * L) ** -0.5, 0.09375, ((0, 32), (1, 16)))
    far_target_keys = jax.random.split(jax.random.fold_in(key_list[3], 1), TA * TB * L // L)
    far_target_turns = jax.random.permutation(jax.random.fold_in(key_list[3], 3), TA * TB * L // L)
    far_target = jax.vmap(lambda own, number: routed_block(jax.random.fold_in(key_list[3], 2), own, number, L, TA, 1, CAP, 2))(far_target_keys, far_target_turns).reshape((TA, TB, L, 1))
    far_delay = touch_ends(jax.random.randint(key_list[4], (TA, TB, L), 1, K + 1), jax.random.fold_in(key_list[4], 1), 1, K).astype(jnp.int32)
    near_blocks = centred(key_list[5], (TA, TB, 3, SEG, SEG), (SEG * 12) ** -0.5, 0.15625, ((0, 32), (1, 16)))
    near_link = touch_ends((jax.random.randint(key_list[6], (TA, TB, 2), 0, 4) < 3).astype(jnp.int32), jax.random.fold_in(key_list[6], 1), 0, 1)
    jacobi_blocks = centred(key_list[7], (TA, TB, SEG, SEG), (SEG * 6) ** -0.5, 0.21875, ((0, 32), (1, 16)))
    return {"voltage": voltage, "history": history, "far_blocks": far_blocks, "far_target": far_target, "far_delay": far_delay, "near_blocks": near_blocks, "near_link": near_link, "jacobi_blocks": jacobi_blocks}


def near_apply(field, near_blocks, near_link):
    blocks_f32 = near_blocks.astype(jnp.float32)
    link_gain = near_link.astype(jnp.float32)
    zero_rim = jnp.zeros_like(field[:, :1])
    lower_side = jnp.concatenate([zero_rim, field[:, :-1]], axis=1)
    upper_side = jnp.concatenate([field[:, 1:], zero_rim], axis=1)
    result = field + jnp.einsum('abcs,abst->abct', field, blocks_f32[:, :, 1], precision=lax.Precision.HIGHEST)
    result = result + link_gain[:, :, 0, None, None] * jnp.einsum('abcs,abst->abct', lower_side, blocks_f32[:, :, 0], precision=lax.Precision.HIGHEST)
    result = result + link_gain[:, :, 1, None, None] * jnp.einsum('abcs,abst->abct', upper_side, blocks_f32[:, :, 2], precision=lax.Precision.HIGHEST)
    return result

def jacobi_apply(field, jacobi_blocks):
    return field + jnp.einsum('abcs,abst->abct', field, jacobi_blocks.astype(jnp.float32), precision=lax.Precision.HIGHEST)

def givens_solve(hessen, start_norm, iterations):
    matrix = [[hessen[i][k] for k in range(iterations)] for i in range(iterations + 1)]
    target = [start_norm] + [jnp.zeros_like(start_norm) for k in range(iterations)]
    for j in range(iterations):
        diag_val = matrix[j][j]
        below_val = matrix[j + 1][j]
        radius = jnp.sqrt(diag_val * diag_val + below_val * below_val)
        cosine = diag_val / radius
        sine_val = below_val / radius
        for k in range(j, iterations):
            upper_val = matrix[j][k]
            lower_val = matrix[j + 1][k]
            matrix[j][k] = cosine * upper_val + sine_val * lower_val
            matrix[j + 1][k] = cosine * lower_val - sine_val * upper_val
        target[j + 1] = -sine_val * target[j]
        target[j] = cosine * target[j]
    coeffs = [None] * iterations
    for j in reversed(range(iterations)):
        partial_val = target[j]
        for k in range(j + 1, iterations):
            partial_val = partial_val - matrix[j][k] * coeffs[k]
        coeffs[j] = partial_val / matrix[j][j]
    return coeffs

def krylov_solve(right_side, near_blocks, near_link, jacobi_blocks):
    initial = jacobi_apply(right_side, jacobi_blocks)
    start_norm = jnp.sqrt(lax.optimization_barrier(jnp.sum(initial * initial, axis=(0, 1, 3))))
    basis = [initial / start_norm[None, None, :, None]]
    zero_row = jnp.zeros_like(start_norm)
    hessen = [[zero_row for k in range(ITERS)] for i in range(ITERS + 1)]
    for j in range(ITERS):
        candidate = jacobi_apply(near_apply(basis[j], near_blocks, near_link), jacobi_blocks)
        projections = [lax.optimization_barrier(jnp.sum(v * candidate, axis=(0, 1, 3))) for v in basis]
        for i in range(j + 1):
            candidate = candidate - projections[i][None, None, :, None] * basis[i]
        new_norm = jnp.sqrt(lax.optimization_barrier(jnp.sum(candidate * candidate, axis=(0, 1, 3))))
        for i in range(j + 1):
            hessen[i][j] = projections[i]
        hessen[j + 1][j] = new_norm
        basis.append(candidate / new_norm[None, None, :, None])
    coeffs = givens_solve(hessen, start_norm, ITERS)
    result = coeffs[0][None, None, :, None] * basis[0]
    for j in range(1, ITERS):
        result = result + coeffs[j][None, None, :, None] * basis[j]
    return result

def far_sum(stacked, far_blocks, far_target, far_delay):
    tiles_a = far_blocks.shape[0]
    tiles_b = far_blocks.shape[1]

    def per_row(b):
        source = stacked[:, b]
        blocks = far_blocks[:, b]
        targets = far_target[:, b, :, 0]
        delays = far_delay[:, b]
        chosen = source[jnp.arange(tiles_a, dtype=jnp.int32)[:, None], (delays - 1).astype(jnp.int32)]
        products = jnp.einsum('alcs,alst->alct', chosen.astype(jnp.float32), blocks.astype(jnp.float32), precision=lax.Precision.HIGHEST)
        gathered = jnp.zeros((tiles_a, products.shape[2], products.shape[3]), jnp.float32)
        return gathered.at[targets].add(products)
    per_rows = lax.map(per_row, jnp.arange(tiles_b, dtype=jnp.int32))
    return jnp.transpose(per_rows, (1, 0, 2, 3))

def reference(voltage, history, far_blocks, far_target, far_delay, near_blocks, near_link, jacobi_blocks):
    currents = []
    for n in range(STEPS):
        pieces = [c.astype(jnp.bfloat16)[:, :, None] for c in reversed(currents)]
        stacked = lax.optimization_barrier(jnp.concatenate(pieces + [history], axis=2))
        far_field = far_sum(stacked, far_blocks, far_target, far_delay)
        right_side = voltage[:, :, n] - far_field
        currents.append(krylov_solve(right_side, near_blocks, near_link, jacobi_blocks))
    return jnp.stack(currents, axis=2)
```

```python
import functools

import jax
import jax.numpy as jnp
from jax import lax
from jax.experimental import pallas as pl
from jax.experimental.pallas import tpu as pltpu
from jax.sharding import PartitionSpec as P

ITERS = 5
BASIS = ITERS + 1
PAIRS = [(i, j) for i in range(BASIS) for j in range(i, BASIS)]
PIVOT_SHARE = 0.02
VMEM_BYTES = 48 * 1024 * 1024
PRECISE = lax.Precision.HIGHEST


def call(kernel, out_shape, in_spaces, **kwargs):
    spaces = {"v": pltpu.VMEM, "s": pltpu.SMEM}
    return pl.pallas_call(
        kernel,
        out_shape=out_shape,
        in_specs=[pl.BlockSpec(memory_space=spaces[c]) for c in in_spaces],
        compiler_params=pltpu.CompilerParams(vmem_limit_bytes=VMEM_BYTES),
        **kwargs,
    )


def split_dot(field, block):
    rows = field.shape[0]
    high = field.astype(jnp.bfloat16)
    low = (field - high.astype(jnp.float32)).astype(jnp.bfloat16)
    both = jnp.dot(jnp.concatenate([high, low], axis=0), block, preferred_element_type=jnp.float32)
    return both[:rows] + both[rows:]


def far_kernel(target_ref, delay_ref, history_ref, blocks_ref, out_ref):
    out_ref[...] = jnp.zeros_like(out_ref)
    for entry in range(blocks_ref.shape[0]):
        target = target_ref[entry]
        product = jnp.dot(
            history_ref[delay_ref[entry] - 1],
            blocks_ref[entry],
            preferred_element_type=jnp.float32,
        )
        out_ref[target] = out_ref[target] + product


def start_kernel(received_ref, voltage_ref, jacobi_ref, out_ref):
    right_side = voltage_ref[...] - jnp.sum(received_ref[...], axis=0)
    out_ref[...] = right_side + split_dot(right_side, jacobi_ref[...])


def power_kernel(link_ref, field_ref, lower_ref, upper_ref, near_ref, jacobi_ref, out_ref):
    field = field_ref[...]
    lower = link_ref[0].astype(jnp.float32) * lower_ref[...]
    upper = link_ref[1].astype(jnp.float32) * upper_ref[...]
    depth = near_ref.shape[0] * near_ref.shape[1]
    near = split_dot(
        jnp.concatenate([lower, field, upper], axis=1), near_ref[...].reshape(depth, field.shape[1])
    )
    out_ref[...] = near + split_dot(field + near, jacobi_ref[...])


def gram_kernel(*refs):
    out_ref = refs[-1]
    fields = [ref[...] for ref in refs[:-1]]
    scenarios, segments = fields[0].shape
    ones = jnp.ones((8, segments), jnp.float32)
    stacked = jnp.concatenate([fields[i] * fields[j] for i, j in PAIRS], axis=0)
    sums = lax.dot_general(
        ones, stacked, (((1,), (1,)), ((), ())), precision=PRECISE, preferred_element_type=jnp.float32
    )
    sums = jnp.concatenate([sums[0:1], jnp.zeros((1, out_ref.shape[2] - sums.shape[1]), jnp.float32)], axis=1)
    out_ref[...] = jnp.broadcast_to(sums[None], out_ref.shape)


def add_kernel(received_ref, out_ref):
    total = jnp.sum(received_ref[...], axis=0)
    out_ref[...] = jnp.broadcast_to(total[None], out_ref.shape)


def solve_kernel(*refs):
    received_ref, field_refs, out_ref, safe_ref = refs[0], refs[1:-2], refs[-2], refs[-1]
    total = jnp.sum(received_ref[...], axis=0)
    scenarios = out_ref.shape[0]
    gram = {pair: total[:, p * scenarios : (p + 1) * scenarios] for p, pair in enumerate(PAIRS)}
    factor = {}
    safe = jnp.ones((1, scenarios), jnp.float32)
    for i in range(BASIS):
        pivot = gram[i, i]
        for k in range(i):
            pivot = pivot - factor[k, i] * factor[k, i]
        safe = jnp.where(pivot >= PIVOT_SHARE * gram[i, i], safe, 0.0)
        safe = jnp.where(pivot > 0.0, safe, 0.0)
        safe = jnp.where(gram[i, i] < jnp.inf, safe, 0.0)
        factor[i, i] = jnp.sqrt(pivot)
        for j in range(i + 1, BASIS):
            entry = gram[i, j]
            for k in range(i):
                entry = entry - factor[k, i] * factor[k, j]
            factor[i, j] = entry / factor[i, i]
    matrix = [[None] * ITERS for _ in range(BASIS)]
    for j in range(ITERS):
        for i in range(j + 1):
            matrix[i][j] = factor[i, j] + factor[i, j + 1]
        matrix[j + 1][j] = factor[j + 1, j + 1]
    target = [factor[0, 0]] + [None] * ITERS
    for j in range(ITERS):
        diagonal, below = matrix[j][j], matrix[j + 1][j]
        radius = jnp.sqrt(diagonal * diagonal + below * below)
        cosine, sine = diagonal / radius, below / radius
        matrix[j][j] = radius
        for k in range(j + 1, ITERS):
            upper, lower = matrix[j][k], matrix[j + 1][k]
            matrix[j][k] = cosine * upper + sine * lower
            matrix[j + 1][k] = cosine * lower - sine * upper
        target[j + 1] = -sine * target[j]
        target[j] = cosine * target[j]
    coeffs = [None] * ITERS
    for j in reversed(range(ITERS)):
        partial = target[j]
        for k in range(j + 1, ITERS):
            partial = partial - matrix[j][k] * coeffs[k]
        coeffs[j] = partial / matrix[j][j]
    padded = jnp.concatenate(coeffs + [jnp.zeros((8 - ITERS, scenarios), jnp.float32)], axis=0)
    padded = jnp.concatenate([padded, jnp.zeros((8, 128 - scenarios), jnp.float32)], axis=1)
    columns = jnp.transpose(padded)[:scenarios]
    result = columns[:, 0:1] * field_refs[0][...]
    for j in range(1, ITERS):
        result = result + columns[:, j : j + 1] * field_refs[j][...]
    out_ref[...] = result
    safe_ref[0] = jnp.min(safe)


def neighbours(field):
    size = lax.axis_size("row")
    up = [(i, i + 1) for i in range(size - 1)]
    down = [(j, i) for i, j in up]
    return lax.ppermute(field, "row", up), lax.ppermute(field, "row", down)


def near_apply(field, near_f32, link_gain):
    lower, upper = neighbours(field)
    result = field + jnp.dot(field, near_f32[1], precision=PRECISE)
    result = result + link_gain[0] * jnp.dot(lower, near_f32[0], precision=PRECISE)
    return result + link_gain[1] * jnp.dot(upper, near_f32[2], precision=PRECISE)


def jacobi_apply(field, jacobi_f32):
    return field + jnp.dot(field, jacobi_f32, precision=PRECISE)


def givens_solve(hessen, start_norm):
    matrix = [[hessen[i][k] for k in range(ITERS)] for i in range(ITERS + 1)]
    target = [start_norm] + [jnp.zeros_like(start_norm) for k in range(ITERS)]
    for j in range(ITERS):
        diag_val = matrix[j][j]
        below_val = matrix[j + 1][j]
        radius = jnp.sqrt(diag_val * diag_val + below_val * below_val)
        cosine = diag_val / radius
        sine_val = below_val / radius
        for k in range(j, ITERS):
            upper_val = matrix[j][k]
            lower_val = matrix[j + 1][k]
            matrix[j][k] = cosine * upper_val + sine_val * lower_val
            matrix[j + 1][k] = cosine * lower_val - sine_val * upper_val
        target[j + 1] = -sine_val * target[j]
        target[j] = cosine * target[j]
    coeffs = [None] * ITERS
    for j in reversed(range(ITERS)):
        partial_val = target[j]
        for k in range(j + 1, ITERS):
            partial_val = partial_val - matrix[j][k] * coeffs[k]
        coeffs[j] = partial_val / matrix[j][j]
    return coeffs


def stepwise_solve(initial, near, jacobi, link):
    near_f32 = near.astype(jnp.float32)
    jacobi_f32 = jacobi.astype(jnp.float32)
    link_gain = link.astype(jnp.float32)
    start_norm = jnp.sqrt(lax.psum(jnp.sum(initial * initial, axis=1), ("tile", "row")))
    basis = [initial / start_norm[:, None]]
    zero_row = jnp.zeros_like(start_norm)
    hessen = [[zero_row for k in range(ITERS)] for i in range(ITERS + 1)]
    for j in range(ITERS):
        candidate = jacobi_apply(near_apply(basis[j], near_f32, link_gain), jacobi_f32)
        local_dots = jnp.stack([jnp.sum(v * candidate, axis=1) for v in basis])
        projections = lax.psum(local_dots, ("tile", "row"))
        for i in range(j + 1):
            candidate = candidate - projections[i][:, None] * basis[i]
        new_norm = jnp.sqrt(lax.psum(jnp.sum(candidate * candidate, axis=1), ("tile", "row")))
        for i in range(j + 1):
            hessen[i][j] = projections[i]
        hessen[j + 1][j] = new_norm
        basis.append(candidate / new_norm[:, None])
    coeffs = givens_solve(hessen, start_norm)
    result = coeffs[0][:, None] * basis[0]
    for j in range(1, ITERS):
        result = result + coeffs[j][:, None] * basis[j]
    return result


def per_device(
    voltage, history, far_blocks, far_target, far_delay, near_blocks, near_link, jacobi_blocks
):
    voltage = voltage[0, 0, 0]
    history = history[0, 0]
    far_blocks = far_blocks[0, 0]
    targets = far_target[0, 0, :, 0]
    delays = far_delay[0, 0]
    near = near_blocks[0, 0]
    link = near_link[0, 0]
    jacobi = jacobi_blocks[0, 0]
    tiles, rows = lax.axis_size("tile"), lax.axis_size("row")
    scenarios, segments = voltage.shape
    f32 = jnp.float32
    field_shape = jax.ShapeDtypeStruct((scenarios, segments), f32)

    bucket = call(
        far_kernel, jax.ShapeDtypeStruct((tiles, scenarios, segments), f32), "ssvv"
    )(targets, delays, history, far_blocks)
    received = lax.all_to_all(bucket, "tile", split_axis=0, concat_axis=0, tiled=True)
    initial = call(start_kernel, field_shape, "vvv")(received, voltage, jacobi)

    power = call(power_kernel, field_shape, "svvvvv")
    fields = [initial]
    for _ in range(ITERS):
        lower, upper = neighbours(fields[-1])
        fields.append(power(link, fields[-1], lower, upper, near, jacobi))

    width = -(-len(PAIRS) * scenarios // 128) * 128
    local = call(gram_kernel, jax.ShapeDtypeStruct((rows, 1, width), f32), "v" * BASIS)(*fields)
    by_row = lax.all_to_all(local, "row", split_axis=0, concat_axis=0, tiled=True)
    group = call(add_kernel, jax.ShapeDtypeStruct((tiles, 1, width), f32), "v")(by_row)
    by_tile = lax.all_to_all(group, "tile", split_axis=0, concat_axis=0, tiled=True)
    result, safe = call(
        solve_kernel,
        (field_shape, jax.ShapeDtypeStruct((1,), f32)),
        "v" * (BASIS),
        out_specs=(pl.BlockSpec(memory_space=pltpu.VMEM), pl.BlockSpec(memory_space=pltpu.SMEM)),
    )(by_tile, *fields[:ITERS])
    result = lax.cond(
        safe[0] > 0.5,
        lambda: result,
        lambda: stepwise_solve(initial, near, jacobi, link),
    )
    return result[None, None, None]


def solution(mesh):
    return jax.shard_map(
        per_device,
        mesh=mesh,
        in_specs=(
            P("tile", "row", None, None, None),
            P("tile", "row", None, None, None),
            P("tile", "row", None, None, None),
            P("tile", "row", None, None),
            P("tile", "row", None),
            P("tile", "row", None, None, None),
            P("tile", "row", None),
            P("tile", "row", None, None),
        ),
        out_specs=P("tile", "row", None, None, None),
        check_vma=False,
    )
```

```python
import jax
import jax.numpy as jnp
from jax import lax
from jax.experimental import pallas as pl
from jax.experimental.pallas import tpu as pltpu
from jax.sharding import PartitionSpec as P

ITERS = 5
BASIS = ITERS + 1
PAIRS = [(i, j) for i in range(BASIS) for j in range(i, BASIS)]
PIVOT_SHARE = 0.02
VMEM_BYTES = 48 * 1024 * 1024
PRECISE = lax.Precision.HIGHEST


def call(kernel, out_shape, in_spaces, **kwargs):
    spaces = {"v": pltpu.VMEM, "s": pltpu.SMEM}
    return pl.pallas_call(
        kernel,
        out_shape=out_shape,
        in_specs=[pl.BlockSpec(memory_space=spaces[c]) for c in in_spaces],
        compiler_params=pltpu.CompilerParams(vmem_limit_bytes=VMEM_BYTES),
        **kwargs,
    )


def split_dot(field, block):
    rows = field.shape[0]
    high = field.astype(jnp.bfloat16)
    low = (field - high.astype(jnp.float32)).astype(jnp.bfloat16)
    both = jnp.dot(jnp.concatenate([high, low], axis=0), block, preferred_element_type=jnp.float32)
    return both[:rows] + both[rows:]


def far_kernel(target_ref, delay_ref, history_ref, blocks_ref, out_ref):
    out_ref[...] = jnp.zeros_like(out_ref)
    for entry in range(blocks_ref.shape[0]):
        target = target_ref[entry]
        product = jnp.dot(
            history_ref[delay_ref[entry] - 1],
            blocks_ref[entry],
            preferred_element_type=jnp.float32,
        )
        out_ref[target] = out_ref[target] + product


def start_kernel(received_ref, voltage_ref, jacobi_ref, out_ref):
    right_side = voltage_ref[...] - jnp.sum(received_ref[...], axis=0)
    out_ref[...] = right_side + split_dot(right_side, jacobi_ref[...])


def krylov_kernel(place_ref, start_ref, blocks_ref, gram_ref, own_ref, fields, parts, blocks, sums):
    rows, scenarios, segments = start_ref.shape
    depth = blocks.shape[1]
    zero_part = jnp.zeros(parts.shape[2:], parts.dtype)
    for side in range(2):
        parts[side, 0] = zero_part
        parts[side, rows + 1] = zero_part

    def halves(value):
        high = value.astype(jnp.bfloat16)
        low = (value - high.astype(jnp.float32)).astype(jnp.bfloat16)
        return jnp.concatenate([high, low], axis=0)

    for b in range(rows):
        blocks[b] = blocks_ref[b].reshape(depth, segments).astype(jnp.bfloat16)
        fields[0, b] = start_ref[b]
        parts[0, b + 1] = halves(start_ref[b])

    def power(k, carry):
        now, later = lax.rem(k, 2), lax.rem(k + 1, 2)
        for b in range(rows):
            around = jnp.concatenate([parts[now, b], parts[now, b + 1], parts[now, b + 2]], axis=1)
            near = jnp.dot(
                around, blocks[b, : depth - segments], preferred_element_type=jnp.float32
            )
            near = near[:scenarios] + near[scenarios:]
            last = jnp.dot(
                halves(fields[k, b] + near),
                blocks[b, depth - segments :],
                preferred_element_type=jnp.float32,
            )
            value = near + last[:scenarios] + last[scenarios:]
            fields[k + 1, b] = value
            parts[later, b + 1] = halves(value)
        return carry

    lax.fori_loop(0, ITERS, power, 0)

    def gram(c, carry):
        at = pl.ds(pl.multiple_of(c * 8, 8), 8)
        totals = [jnp.zeros((8, segments), jnp.float32) for _ in PAIRS]
        for b in range(rows):
            values = [fields[i, b, at] for i in range(BASIS)]
            totals = [t + values[i] * values[j] for t, (i, j) in zip(totals, PAIRS)]
        for p, t in enumerate(totals):
            sums[p, at] = t
        return carry

    lax.fori_loop(0, scenarios // 8, gram, 0)
    for p in range(len(PAIRS), sums.shape[0]):
        sums[p] = jnp.zeros((scenarios, segments), jnp.float32)
    total = lax.dot_general(
        jnp.ones((8, segments), jnp.float32),
        sums[...].reshape(sums.shape[0] * scenarios, segments),
        (((1,), (1,)), ((), ())),
        precision=PRECISE,
        preferred_element_type=jnp.float32,
    )
    gram_ref[...] = jnp.broadcast_to(total[0:1][None], gram_ref.shape)
    for j in range(ITERS):
        own_ref[j] = fields[j, place_ref[0]]


def solve_kernel(received_ref, fields_ref, out_ref, safe_ref):
    total = jnp.sum(received_ref[...], axis=0)
    scenarios = out_ref.shape[0]
    gram = {pair: total[:, p * scenarios : (p + 1) * scenarios] for p, pair in enumerate(PAIRS)}
    factor = {}
    safe = jnp.ones((1, scenarios), jnp.float32)
    for i in range(BASIS):
        pivot = gram[i, i]
        for k in range(i):
            pivot = pivot - factor[k, i] * factor[k, i]
        safe = jnp.where(pivot >= PIVOT_SHARE * gram[i, i], safe, 0.0)
        safe = jnp.where(pivot > 0.0, safe, 0.0)
        safe = jnp.where(gram[i, i] < jnp.inf, safe, 0.0)
        factor[i, i] = jnp.sqrt(pivot)
        for j in range(i + 1, BASIS):
            entry = gram[i, j]
            for k in range(i):
                entry = entry - factor[k, i] * factor[k, j]
            factor[i, j] = entry / factor[i, i]
    matrix = [[None] * ITERS for _ in range(BASIS)]
    for j in range(ITERS):
        for i in range(j + 1):
            matrix[i][j] = factor[i, j] + factor[i, j + 1]
        matrix[j + 1][j] = factor[j + 1, j + 1]
    target = [factor[0, 0]] + [None] * ITERS
    for j in range(ITERS):
        diagonal, below = matrix[j][j], matrix[j + 1][j]
        radius = jnp.sqrt(diagonal * diagonal + below * below)
        cosine, sine = diagonal / radius, below / radius
        matrix[j][j] = radius
        for k in range(j + 1, ITERS):
            upper, lower = matrix[j][k], matrix[j + 1][k]
            matrix[j][k] = cosine * upper + sine * lower
            matrix[j + 1][k] = cosine * lower - sine * upper
        target[j + 1] = -sine * target[j]
        target[j] = cosine * target[j]
    coeffs = [None] * ITERS
    for j in reversed(range(ITERS)):
        partial = target[j]
        for k in range(j + 1, ITERS):
            partial = partial - matrix[j][k] * coeffs[k]
        coeffs[j] = partial / matrix[j][j]
    padded = jnp.concatenate(coeffs + [jnp.zeros((8 - ITERS, scenarios), jnp.float32)], axis=0)
    padded = jnp.concatenate([padded, jnp.zeros((8, 128 - scenarios), jnp.float32)], axis=1)
    columns = jnp.transpose(padded)[:scenarios]
    result = columns[:, 0:1] * fields_ref[0]
    for j in range(1, ITERS):
        result = result + columns[:, j : j + 1] * fields_ref[j]
    out_ref[...] = result
    safe_ref[0] = jnp.min(safe)


def neighbours(field):
    size = lax.axis_size("row")
    up = [(i, i + 1) for i in range(size - 1)]
    down = [(j, i) for i, j in up]
    return lax.ppermute(field, "row", up), lax.ppermute(field, "row", down)


def near_apply(field, near_f32, link_gain):
    lower, upper = neighbours(field)
    result = field + jnp.dot(field, near_f32[1], precision=PRECISE)
    result = result + link_gain[0] * jnp.dot(lower, near_f32[0], precision=PRECISE)
    return result + link_gain[1] * jnp.dot(upper, near_f32[2], precision=PRECISE)


def jacobi_apply(field, jacobi_f32):
    return field + jnp.dot(field, jacobi_f32, precision=PRECISE)


def givens_solve(hessen, start_norm):
    matrix = [[hessen[i][k] for k in range(ITERS)] for i in range(ITERS + 1)]
    target = [start_norm] + [jnp.zeros_like(start_norm) for k in range(ITERS)]
    for j in range(ITERS):
        diag_val = matrix[j][j]
        below_val = matrix[j + 1][j]
        radius = jnp.sqrt(diag_val * diag_val + below_val * below_val)
        cosine = diag_val / radius
        sine_val = below_val / radius
        for k in range(j, ITERS):
            upper_val = matrix[j][k]
            lower_val = matrix[j + 1][k]
            matrix[j][k] = cosine * upper_val + sine_val * lower_val
            matrix[j + 1][k] = cosine * lower_val - sine_val * upper_val
        target[j + 1] = -sine_val * target[j]
        target[j] = cosine * target[j]
    coeffs = [None] * ITERS
    for j in reversed(range(ITERS)):
        partial_val = target[j]
        for k in range(j + 1, ITERS):
            partial_val = partial_val - matrix[j][k] * coeffs[k]
        coeffs[j] = partial_val / matrix[j][j]
    return coeffs


def stepwise_solve(initial, near, jacobi, link):
    near_f32 = near.astype(jnp.float32)
    jacobi_f32 = jacobi.astype(jnp.float32)
    link_gain = link.astype(jnp.float32)
    start_norm = jnp.sqrt(lax.psum(jnp.sum(initial * initial, axis=1), ("tile", "row")))
    basis = [initial / start_norm[:, None]]
    zero_row = jnp.zeros_like(start_norm)
    hessen = [[zero_row for k in range(ITERS)] for i in range(ITERS + 1)]
    for j in range(ITERS):
        candidate = jacobi_apply(near_apply(basis[j], near_f32, link_gain), jacobi_f32)
        local_dots = jnp.stack([jnp.sum(v * candidate, axis=1) for v in basis])
        projections = lax.psum(local_dots, ("tile", "row"))
        for i in range(j + 1):
            candidate = candidate - projections[i][:, None] * basis[i]
        new_norm = jnp.sqrt(lax.psum(jnp.sum(candidate * candidate, axis=1), ("tile", "row")))
        for i in range(j + 1):
            hessen[i][j] = projections[i]
        hessen[j + 1][j] = new_norm
        basis.append(candidate / new_norm[:, None])
    coeffs = givens_solve(hessen, start_norm)
    result = coeffs[0][:, None] * basis[0]
    for j in range(1, ITERS):
        result = result + coeffs[j][:, None] * basis[j]
    return result


def per_device(
    voltage, history, far_blocks, far_target, far_delay, near_blocks, near_link, jacobi_blocks
):
    voltage = voltage[0, 0, 0]
    history = history[0, 0]
    far_blocks = far_blocks[0, 0]
    targets = far_target[0, 0, :, 0]
    delays = far_delay[0, 0]
    near = near_blocks[0, 0]
    link = near_link[0, 0]
    jacobi = jacobi_blocks[0, 0]
    tiles, rows = lax.axis_size("tile"), lax.axis_size("row")
    scenarios, segments = voltage.shape
    f32 = jnp.float32
    field_shape = jax.ShapeDtypeStruct((scenarios, segments), f32)

    gate = jnp.stack([link[0], jnp.ones_like(link[0]), link[1]]).astype(f32)
    own_blocks = jnp.concatenate(
        [near.astype(f32) * gate[:, None, None], jacobi.astype(f32)[None]], axis=0
    )
    all_blocks = lax.all_gather(own_blocks, "row")

    bucket = call(
        far_kernel, jax.ShapeDtypeStruct((tiles, scenarios, segments), f32), "ssvv"
    )(targets, delays, history, far_blocks)
    received = lax.all_to_all(bucket, "tile", split_axis=0, concat_axis=0, tiled=True)
    initial = call(start_kernel, field_shape, "vvv")(received, voltage, jacobi)

    starts = lax.all_gather(initial, "row")

    padded_pairs = -(-len(PAIRS) * scenarios // 128) * 128 // scenarios
    width = padded_pairs * scenarios
    gram, own = call(
        krylov_kernel,
        (
            jax.ShapeDtypeStruct((tiles, 1, width), f32),
            jax.ShapeDtypeStruct((ITERS, scenarios, segments), f32),
        ),
        "svv",
        scratch_shapes=[
            pltpu.VMEM((BASIS, rows, scenarios, segments), f32),
            pltpu.VMEM((2, rows + 2, 2 * scenarios, segments), jnp.bfloat16),
            pltpu.VMEM((rows, 4 * segments, segments), jnp.bfloat16),
            pltpu.VMEM((padded_pairs, scenarios, segments), f32),
        ],
    )(lax.axis_index("row").astype(jnp.int32)[None], starts, all_blocks)
    by_tile = lax.all_to_all(gram, "tile", split_axis=0, concat_axis=0, tiled=True)
    result, safe = call(
        solve_kernel,
        (field_shape, jax.ShapeDtypeStruct((1,), f32)),
        "vv",
        out_specs=(pl.BlockSpec(memory_space=pltpu.VMEM), pl.BlockSpec(memory_space=pltpu.SMEM)),
    )(by_tile, own)
    result = lax.cond(
        safe[0] > 0.5,
        lambda: result,
        lambda: stepwise_solve(initial, near, jacobi, link),
    )
    return result[None, None, None]


def solution(mesh):
    return jax.shard_map(
        per_device,
        mesh=mesh,
        in_specs=(
            P("tile", "row", None, None, None),
            P("tile", "row", None, None, None),
            P("tile", "row", None, None, None),
            P("tile", "row", None, None),
            P("tile", "row", None),
            P("tile", "row", None, None, None),
            P("tile", "row", None),
            P("tile", "row", None, None),
        ),
        out_specs=P("tile", "row", None, None, None),
        check_vma=False,
    )
```

```python
import jax
import jax.numpy as jnp
from jax import lax
from jax.experimental import pallas as pl
from jax.experimental.pallas import tpu as pltpu
from jax.sharding import PartitionSpec as P

ITERS = 5
BASIS = ITERS + 1
PAIRS = [(i, j) for i in range(BASIS) for j in range(i, BASIS)]
PIVOT_SHARE = 0.02
VMEM_BYTES = 48 * 1024 * 1024
PRECISE = lax.Precision.HIGHEST


def call(kernel, out_shape, in_spaces, **kwargs):
    spaces = {"v": pltpu.VMEM, "s": pltpu.SMEM, "h": pltpu.HBM}
    run = pl.pallas_call(
        kernel,
        out_shape=out_shape,
        in_specs=[pl.BlockSpec(memory_space=spaces[c]) for c in in_spaces],
        compiler_params=pltpu.CompilerParams(vmem_limit_bytes=VMEM_BYTES),
        **kwargs,
    )

    def placed(*operands):
        return run(
            *(
                pltpu.with_memory_space_constraint(x, pltpu.HBM) if c == "h" else x
                for c, x in zip(in_spaces, operands)
            )
        )

    return placed


def split_dot(field, block):
    rows = field.shape[0]
    high = field.astype(jnp.bfloat16)
    low = (field - high.astype(jnp.float32)).astype(jnp.bfloat16)
    both = jnp.dot(jnp.concatenate([high, low], axis=0), block, preferred_element_type=jnp.float32)
    return both[:rows] + both[rows:]


def front_kernel(
    target_hbm, delay_hbm, link_hbm, near_hbm, jacobi_hbm, history_hbm, blocks_hbm, bucket_ref, own_ref,
    target_ref, delay_ref, link_ref, near_ref, jacobi_ref, history_ref, blocks_ref, sems, block_sems,
):
    entries, chunks = blocks_ref.shape[0], block_sems.shape[0]
    step = entries // chunks
    pairs = [
        (target_hbm, target_ref), (delay_hbm, delay_ref), (link_hbm, link_ref),
        (near_hbm, near_ref), (jacobi_hbm, jacobi_ref), (history_hbm, history_ref),
    ]
    copies = [pltpu.make_async_copy(a, b, sems.at[i]) for i, (a, b) in enumerate(pairs)]
    slabs = [
        pltpu.make_async_copy(
            blocks_hbm.at[pl.ds(c * step, step)], blocks_ref.at[pl.ds(c * step, step)], block_sems.at[c]
        )
        for c in range(chunks)
    ]
    for copy in copies + slabs:
        copy.start()
    bucket_ref[...] = jnp.zeros_like(bucket_ref)
    for copy in copies:
        copy.wait()
    for side, gate in enumerate((link_ref[0], 1, link_ref[1])):
        own_ref[side] = near_ref[side].astype(jnp.float32) * jnp.float32(gate)
    own_ref[near_ref.shape[0]] = jacobi_ref[...].astype(jnp.float32)
    for c in range(chunks):
        slabs[c].wait()
        for entry in range(c * step, (c + 1) * step):
            target = target_ref[entry]
            product = jnp.dot(
                history_ref[delay_ref[entry] - 1],
                blocks_ref[entry],
                preferred_element_type=jnp.float32,
            )
            bucket_ref[target] = bucket_ref[target] + product


def start_kernel(received_ref, voltage_ref, jacobi_ref, out_ref):
    right_side = voltage_ref[...] - jnp.sum(received_ref[...], axis=0)
    out_ref[...] = right_side + split_dot(right_side, jacobi_ref[...])


def krylov_kernel(
    place_ref, start_ref, blocks_hbm, gram_ref, own_ref, fields, nears, parts, blocks, sums, staged, sems
):
    rows, scenarios, segments = start_ref.shape
    depth, group = blocks.shape[1], rows // 4
    copies = [pltpu.make_async_copy(blocks_hbm.at[b], staged.at[b], sems.at[b]) for b in range(rows)]
    for copy in copies:
        copy.start()
    zero_part = jnp.zeros(parts.shape[2:], parts.dtype)
    for side in range(2):
        parts[side, 0] = zero_part
        parts[side, rows + 1] = zero_part

    def halves(value):
        high = value.astype(jnp.bfloat16)
        low = (value - high.astype(jnp.float32)).astype(jnp.bfloat16)
        return jnp.concatenate([high, low], axis=0)

    for b in range(rows):
        fields[0, b] = start_ref[b]
        parts[0, b + 1] = halves(start_ref[b])

    for k in range(ITERS):
        now, later = k % 2, (k + 1) % 2
        for b in range(rows):
            if k == 0 and b % group == 0:
                for c in range(b, b + group):
                    copies[c].wait()
                for c in range(b, b + group):
                    blocks[c] = staged[c].reshape(depth, segments).astype(jnp.bfloat16)
            around = jnp.concatenate([parts[now, b], parts[now, b + 1], parts[now, b + 2]], axis=1)
            near = jnp.dot(
                around, blocks[b, : depth - segments], preferred_element_type=jnp.float32
            )
            nears[b] = near[:scenarios] + near[scenarios:]
        for b in range(rows):
            last = jnp.dot(
                halves(fields[k, b] + nears[b]),
                blocks[b, depth - segments :],
                preferred_element_type=jnp.float32,
            )
            value = nears[b] + (last[:scenarios] + last[scenarios:])
            fields[k + 1, b] = value
            if k + 1 < ITERS:
                parts[later, b + 1] = halves(value)

    def gram(c, carry):
        at = pl.ds(pl.multiple_of(c * 8, 8), 8)
        totals = [jnp.zeros((8, segments), jnp.float32) for _ in PAIRS]
        for b in range(rows):
            values = [fields[i, b, at] for i in range(BASIS)]
            totals = [t + values[i] * values[j] for t, (i, j) in zip(totals, PAIRS)]
        for p, t in enumerate(totals):
            sums[p, at] = t
        return carry

    lax.fori_loop(0, scenarios // 8, gram, 0)
    for p in range(len(PAIRS), sums.shape[0]):
        sums[p] = jnp.zeros((scenarios, segments), jnp.float32)
    total = lax.dot_general(
        jnp.ones((8, segments), jnp.float32),
        sums[...].reshape(sums.shape[0] * scenarios, segments),
        (((1,), (1,)), ((), ())),
        precision=PRECISE,
        preferred_element_type=jnp.float32,
    )
    gram_ref[...] = jnp.broadcast_to(total[0:1][None], gram_ref.shape)
    for j in range(ITERS):
        own_ref[j] = fields[j, place_ref[0]]


def krylov_call(place, starts, blocks, tiles=32):
    rows, scenarios, segments = starts.shape
    f32 = jnp.float32
    padded_pairs = -(-len(PAIRS) * scenarios // 128) * 128 // scenarios
    return call(
        krylov_kernel,
        (
            jax.ShapeDtypeStruct((tiles, 1, padded_pairs * scenarios), f32),
            jax.ShapeDtypeStruct((ITERS, scenarios, segments), f32),
        ),
        "svh",
        scratch_shapes=[
            pltpu.VMEM((BASIS, rows, scenarios, segments), f32),
            pltpu.VMEM((rows, scenarios, segments), f32),
            pltpu.VMEM((2, rows + 2, 2 * scenarios, segments), jnp.bfloat16),
            pltpu.VMEM((rows, 4 * segments, segments), jnp.bfloat16),
            pltpu.VMEM((padded_pairs, scenarios, segments), f32),
            pltpu.VMEM(blocks.shape, f32),
            pltpu.SemaphoreType.DMA((rows,)),
        ],
    )(place, starts, blocks)


def solve_kernel(received_ref, fields_ref, out_ref, safe_ref):
    total = jnp.sum(received_ref[...], axis=0)
    scenarios = out_ref.shape[0]
    gram = {pair: total[:, p * scenarios : (p + 1) * scenarios] for p, pair in enumerate(PAIRS)}
    factor = {}
    safe = jnp.ones((1, scenarios), jnp.float32)
    for i in range(BASIS):
        pivot = gram[i, i]
        for k in range(i):
            pivot = pivot - factor[k, i] * factor[k, i]
        safe = jnp.where(pivot >= PIVOT_SHARE * gram[i, i], safe, 0.0)
        safe = jnp.where(pivot > 0.0, safe, 0.0)
        safe = jnp.where(gram[i, i] < jnp.inf, safe, 0.0)
        factor[i, i] = jnp.sqrt(pivot)
        for j in range(i + 1, BASIS):
            entry = gram[i, j]
            for k in range(i):
                entry = entry - factor[k, i] * factor[k, j]
            factor[i, j] = entry / factor[i, i]
    matrix = [[None] * ITERS for _ in range(BASIS)]
    for j in range(ITERS):
        for i in range(j + 1):
            matrix[i][j] = factor[i, j] + factor[i, j + 1]
        matrix[j + 1][j] = factor[j + 1, j + 1]
    target = [factor[0, 0]] + [None] * ITERS
    for j in range(ITERS):
        diagonal, below = matrix[j][j], matrix[j + 1][j]
        radius = jnp.sqrt(diagonal * diagonal + below * below)
        cosine, sine = diagonal / radius, below / radius
        matrix[j][j] = radius
        for k in range(j + 1, ITERS):
            upper, lower = matrix[j][k], matrix[j + 1][k]
            matrix[j][k] = cosine * upper + sine * lower
            matrix[j + 1][k] = cosine * lower - sine * upper
        target[j + 1] = -sine * target[j]
        target[j] = cosine * target[j]
    coeffs = [None] * ITERS
    for j in reversed(range(ITERS)):
        partial = target[j]
        for k in range(j + 1, ITERS):
            partial = partial - matrix[j][k] * coeffs[k]
        coeffs[j] = partial / matrix[j][j]
    padded = jnp.concatenate(coeffs + [jnp.zeros((8 - ITERS, scenarios), jnp.float32)], axis=0)
    padded = jnp.concatenate([padded, jnp.zeros((8, 128 - scenarios), jnp.float32)], axis=1)
    columns = jnp.transpose(padded)[:scenarios]
    result = columns[:, 0:1] * fields_ref[0]
    for j in range(1, ITERS):
        result = result + columns[:, j : j + 1] * fields_ref[j]
    out_ref[...] = result
    safe_ref[0] = jnp.min(safe)


def neighbours(field):
    size = lax.axis_size("row")
    up = [(i, i + 1) for i in range(size - 1)]
    down = [(j, i) for i, j in up]
    return lax.ppermute(field, "row", up), lax.ppermute(field, "row", down)


def near_apply(field, near_f32, link_gain):
    lower, upper = neighbours(field)
    result = field + jnp.dot(field, near_f32[1], precision=PRECISE)
    result = result + link_gain[0] * jnp.dot(lower, near_f32[0], precision=PRECISE)
    return result + link_gain[1] * jnp.dot(upper, near_f32[2], precision=PRECISE)


def jacobi_apply(field, jacobi_f32):
    return field + jnp.dot(field, jacobi_f32, precision=PRECISE)


def givens_solve(hessen, start_norm):
    matrix = [[hessen[i][k] for k in range(ITERS)] for i in range(ITERS + 1)]
    target = [start_norm] + [jnp.zeros_like(start_norm) for k in range(ITERS)]
    for j in range(ITERS):
        diag_val = matrix[j][j]
        below_val = matrix[j + 1][j]
        radius = jnp.sqrt(diag_val * diag_val + below_val * below_val)
        cosine = diag_val / radius
        sine_val = below_val / radius
        for k in range(j, ITERS):
            upper_val = matrix[j][k]
            lower_val = matrix[j + 1][k]
            matrix[j][k] = cosine * upper_val + sine_val * lower_val
            matrix[j + 1][k] = cosine * lower_val - sine_val * upper_val
        target[j + 1] = -sine_val * target[j]
        target[j] = cosine * target[j]
    coeffs = [None] * ITERS
    for j in reversed(range(ITERS)):
        partial_val = target[j]
        for k in range(j + 1, ITERS):
            partial_val = partial_val - matrix[j][k] * coeffs[k]
        coeffs[j] = partial_val / matrix[j][j]
    return coeffs


def stepwise_solve(initial, near, jacobi, link):
    near_f32 = near.astype(jnp.float32)
    jacobi_f32 = jacobi.astype(jnp.float32)
    link_gain = link.astype(jnp.float32)
    start_norm = jnp.sqrt(lax.psum(jnp.sum(initial * initial, axis=1), ("tile", "row")))
    basis = [initial / start_norm[:, None]]
    zero_row = jnp.zeros_like(start_norm)
    hessen = [[zero_row for k in range(ITERS)] for i in range(ITERS + 1)]
    for j in range(ITERS):
        candidate = jacobi_apply(near_apply(basis[j], near_f32, link_gain), jacobi_f32)
        local_dots = jnp.stack([jnp.sum(v * candidate, axis=1) for v in basis])
        projections = lax.psum(local_dots, ("tile", "row"))
        for i in range(j + 1):
            candidate = candidate - projections[i][:, None] * basis[i]
        new_norm = jnp.sqrt(lax.psum(jnp.sum(candidate * candidate, axis=1), ("tile", "row")))
        for i in range(j + 1):
            hessen[i][j] = projections[i]
        hessen[j + 1][j] = new_norm
        basis.append(candidate / new_norm[:, None])
    coeffs = givens_solve(hessen, start_norm)
    result = coeffs[0][:, None] * basis[0]
    for j in range(1, ITERS):
        result = result + coeffs[j][:, None] * basis[j]
    return result


def per_device(
    voltage, history, far_blocks, far_target, far_delay, near_blocks, near_link, jacobi_blocks
):
    voltage = voltage[0, 0, 0]
    history = history[0, 0]
    far_blocks = far_blocks[0, 0]
    targets = far_target[0, 0, :, 0]
    delays = far_delay[0, 0]
    near = near_blocks[0, 0]
    link = near_link[0, 0]
    jacobi = jacobi_blocks[0, 0]
    tiles, rows = lax.axis_size("tile"), lax.axis_size("row")
    scenarios, segments = voltage.shape
    f32 = jnp.float32
    field_shape = jax.ShapeDtypeStruct((scenarios, segments), f32)

    inputs = (targets, delays, link, near, jacobi, history, far_blocks)
    spaces = [pltpu.SMEM] * 3 + [pltpu.VMEM] * 4
    bucket, own_blocks = call(
        front_kernel,
        (
            jax.ShapeDtypeStruct((tiles, scenarios, segments), f32),
            jax.ShapeDtypeStruct((near.shape[0] + 1, segments, segments), f32),
        ),
        "h" * len(inputs),
        scratch_shapes=[space(x.shape, x.dtype) for space, x in zip(spaces, inputs)]
        + [pltpu.SemaphoreType.DMA((len(inputs) - 1,)), pltpu.SemaphoreType.DMA((4,))],
    )(*inputs)
    all_blocks = lax.all_gather(own_blocks, "row")
    received = lax.all_to_all(bucket, "tile", split_axis=0, concat_axis=0, tiled=True)
    initial = call(start_kernel, field_shape, "vvv")(received, voltage, jacobi)

    starts = lax.all_gather(initial, "row")

    place = lax.axis_index("row").astype(jnp.int32)[None]
    gram, own = krylov_call(place, starts, all_blocks, tiles)
    by_tile = lax.all_to_all(gram, "tile", split_axis=0, concat_axis=0, tiled=True)
    result, safe = call(
        solve_kernel,
        (field_shape, jax.ShapeDtypeStruct((1,), f32)),
        "vv",
        out_specs=(pl.BlockSpec(memory_space=pltpu.VMEM), pl.BlockSpec(memory_space=pltpu.SMEM)),
    )(by_tile, own)
    result = lax.cond(
        safe[0] > 0.5,
        lambda: result,
        lambda: stepwise_solve(initial, near, jacobi, link),
    )
    return result[None, None, None]


def solution(mesh):
    return jax.shard_map(
        per_device,
        mesh=mesh,
        in_specs=(
            P("tile", "row", None, None, None),
            P("tile", "row", None, None, None),
            P("tile", "row", None, None, None),
            P("tile", "row", None, None),
            P("tile", "row", None),
            P("tile", "row", None, None, None),
            P("tile", "row", None),
            P("tile", "row", None, None),
        ),
        out_specs=P("tile", "row", None, None, None),
        check_vma=False,
    )
```

```python
import jax
import jax.numpy as jnp
from jax import lax
from jax.experimental import pallas as pl
from jax.experimental.pallas import tpu as pltpu
from jax.sharding import PartitionSpec as P

ITERS = 5
BASIS = ITERS + 1
PAIRS = [(i, j) for i in range(BASIS) for j in range(i, BASIS)]
PIVOT_SHARE = 0.02
VMEM_BYTES = 20 * 1024 * 1024
PRECISE = lax.Precision.HIGHEST
CORES = 2
CHIPS = 8


def call(kernel, out_shape, in_spaces, **kwargs):
    spaces = {"v": pltpu.VMEM, "s": pltpu.SMEM, "h": pltpu.HBM}
    run = pl.pallas_call(
        kernel,
        out_shape=out_shape,
        in_specs=[pl.BlockSpec(memory_space=spaces[c]) for c in in_spaces],
        compiler_params=pltpu.CompilerParams(vmem_limit_bytes=VMEM_BYTES),
        **kwargs,
    )

    def placed(*operands):
        return run(
            *(
                pltpu.with_memory_space_constraint(x, pltpu.HBM) if c == "h" else x
                for c, x in zip(in_spaces, operands)
            )
        )

    return placed


def split_dot(field, block):
    rows = field.shape[0]
    high = field.astype(jnp.bfloat16)
    low = (field - high.astype(jnp.float32)).astype(jnp.bfloat16)
    both = jnp.dot(jnp.concatenate([high, low], axis=0), block, preferred_element_type=jnp.float32)
    return both[:rows] + both[rows:]


def ring_steps():
    steps = [0]
    for distance in range(1, CHIPS // 2 + 1):
        steps += [distance] if distance == CHIPS // 2 else [distance, -distance]
    return steps


def front_kernel(
    tile_ref, target_hbm, delay_hbm, link_hbm, near_hbm, jacobi_hbm, voltage_hbm, history_hbm, blocks_hbm,
    bucket_ref, own_ref, kept_ref,
    target_ref, delay_ref, link_ref, near_ref, jacobi_ref, voltage_ref, history_ref, blocks_ref, sems, block_sems,
):
    entries, chunks = blocks_ref.shape[0], block_sems.shape[0]
    step = entries // chunks
    pairs = [
        (target_hbm, target_ref), (delay_hbm, delay_ref), (link_hbm, link_ref),
        (near_hbm, near_ref), (jacobi_hbm, jacobi_ref), (voltage_hbm, voltage_ref),
        (history_hbm, history_ref),
    ]
    copies = [pltpu.make_async_copy(a, b, sems.at[i]) for i, (a, b) in enumerate(pairs)]
    slabs = [
        pltpu.make_async_copy(
            blocks_hbm.at[pl.ds(c * step, step)], blocks_ref.at[pl.ds(c * step, step)], block_sems.at[c]
        )
        for c in range(chunks)
    ]
    for copy in copies + slabs:
        copy.start()
    bucket_ref[...] = jnp.zeros_like(bucket_ref)
    for copy in copies:
        copy.wait()
    jacobi = jacobi_ref[...]
    kept_ref[...] = jacobi
    for side, gate in enumerate((link_ref[0], 1, link_ref[1])):
        near = near_ref[side]
        product = jnp.dot(near, jacobi, preferred_element_type=jnp.float32)
        merged = near.astype(jnp.float32) + product
        own_ref[side] = merged + jacobi.astype(jnp.float32) if side == 1 else merged * gate.astype(jnp.float32)
    bucket_ref[tile_ref[0]] = -voltage_ref[...]
    for c in range(chunks):
        slabs[c].wait()
        for entry in range(c * step, (c + 1) * step):
            target = target_ref[entry]
            product = jnp.dot(
                history_ref[delay_ref[entry] - 1],
                blocks_ref[entry],
                preferred_element_type=jnp.float32,
            )
            bucket_ref[target] = bucket_ref[target] + product


def start_kernel(received_ref, jacobi_ref, out_ref):
    right_side = -jnp.sum(received_ref[...], axis=0)
    out_ref[...] = right_side + split_dot(right_side, jacobi_ref[...])


def krylov_kernel(place_ref, start_ref, *refs):
    chips = CHIPS
    piece_refs = refs[:chips]
    gram_ref, own_ref, fields, parts, highs, lows, sums = refs[chips:]
    rows, scenarios, segments = start_ref.shape
    cores = rows // chips
    zero_part = jnp.zeros(parts.shape[2:], parts.dtype)
    for side in range(2):
        parts[side, 0] = zero_part
        parts[side, rows + 1] = zero_part

    def halves(value):
        high = value.astype(jnp.bfloat16)
        low = (value - high.astype(jnp.float32)).astype(jnp.bfloat16)
        return high, low

    chip, core = lax.div(place_ref[0], cores), lax.rem(place_ref[0], cores)
    for piece_ref, steps in zip(piece_refs, ring_steps()):
        source = lax.rem(chip + (2 * core - 1) * steps + chips, chips)
        for core_there in range(cores):
            b = source * cores + core_there
            highs[b], lows[b] = halves(piece_ref[core_there].reshape(highs.shape[1:]))
    for b in range(rows):
        fields[0, b] = start_ref[b]
        parts[0, b + 1] = jnp.concatenate(halves(start_ref[b]), axis=0)

    for k in range(ITERS):
        now, later = k % 2, (k + 1) % 2
        for b in range(rows):
            around = jnp.concatenate([parts[now, b], parts[now, b + 1], parts[now, b + 2]], axis=1)
            main = jnp.dot(around, highs[b], preferred_element_type=jnp.float32)
            rest = jnp.dot(around[:scenarios], lows[b], preferred_element_type=jnp.float32)
            value = main[:scenarios] + (main[scenarios:] + rest)
            fields[k + 1, b] = value
            if k + 1 < ITERS:
                parts[later, b + 1] = jnp.concatenate(halves(value), axis=0)

    def gram(c, carry):
        at = pl.ds(pl.multiple_of(c * 8, 8), 8)
        totals = [jnp.zeros((8, segments), jnp.float32) for _ in PAIRS]
        for b in range(rows):
            values = [fields[i, b, at] for i in range(BASIS)]
            totals = [t + values[i] * values[j] for t, (i, j) in zip(totals, PAIRS)]
        for p, t in enumerate(totals):
            sums[p, at] = t
        return carry

    lax.fori_loop(0, scenarios // 8, gram, 0)
    for p in range(len(PAIRS), sums.shape[0]):
        sums[p] = jnp.zeros((scenarios, segments), jnp.float32)
    total = lax.dot_general(
        jnp.ones((8, segments), jnp.float32),
        sums[...].reshape(sums.shape[0] * scenarios, segments),
        (((1,), (1,)), ((), ())),
        precision=PRECISE,
        preferred_element_type=jnp.float32,
    )
    gram_ref[...] = jnp.broadcast_to(total[0:1][None], gram_ref.shape)
    for j in range(ITERS):
        own_ref[j] = fields[j, place_ref[0]]


def krylov_call(place, starts, pieces, tiles=32):
    rows, scenarios, segments = starts.shape
    f32 = jnp.float32
    padded_pairs = -(-len(PAIRS) * scenarios // 128) * 128 // scenarios
    return call(
        krylov_kernel,
        (
            jax.ShapeDtypeStruct((tiles, 1, padded_pairs * scenarios), f32),
            jax.ShapeDtypeStruct((ITERS, scenarios, segments), f32),
        ),
        "sv" + "v" * len(pieces),
        scratch_shapes=[
            pltpu.VMEM((BASIS, rows, scenarios, segments), f32),
            pltpu.VMEM((2, rows + 2, 2 * scenarios, segments), jnp.bfloat16),
            pltpu.VMEM((rows, 3 * segments, segments), jnp.bfloat16),
            pltpu.VMEM((rows, 3 * segments, segments), jnp.bfloat16),
            pltpu.VMEM((padded_pairs, scenarios, segments), f32),
        ],
    )(place, starts, *pieces)


def solve_kernel(received_ref, fields_ref, out_ref, safe_ref):
    total = jnp.sum(received_ref[...], axis=0)
    scenarios = out_ref.shape[0]
    gram = {pair: total[:, p * scenarios : (p + 1) * scenarios] for p, pair in enumerate(PAIRS)}
    factor = {}
    safe = jnp.ones((1, scenarios), jnp.float32)
    for i in range(BASIS):
        pivot = gram[i, i]
        for k in range(i):
            pivot = pivot - factor[k, i] * factor[k, i]
        safe = jnp.where(pivot >= PIVOT_SHARE * gram[i, i], safe, 0.0)
        safe = jnp.where(pivot > 0.0, safe, 0.0)
        safe = jnp.where(gram[i, i] < jnp.inf, safe, 0.0)
        factor[i, i] = jnp.sqrt(pivot)
        for j in range(i + 1, BASIS):
            entry = gram[i, j]
            for k in range(i):
                entry = entry - factor[k, i] * factor[k, j]
            factor[i, j] = entry / factor[i, i]
    matrix = [[None] * ITERS for _ in range(BASIS)]
    for j in range(ITERS):
        for i in range(j + 1):
            matrix[i][j] = factor[i, j] + factor[i, j + 1]
        matrix[j + 1][j] = factor[j + 1, j + 1]
    target = [factor[0, 0]] + [None] * ITERS
    for j in range(ITERS):
        diagonal, below = matrix[j][j], matrix[j + 1][j]
        radius = jnp.sqrt(diagonal * diagonal + below * below)
        cosine, sine = diagonal / radius, below / radius
        matrix[j][j] = radius
        for k in range(j + 1, ITERS):
            upper, lower = matrix[j][k], matrix[j + 1][k]
            matrix[j][k] = cosine * upper + sine * lower
            matrix[j + 1][k] = cosine * lower - sine * upper
        target[j + 1] = -sine * target[j]
        target[j] = cosine * target[j]
    coeffs = [None] * ITERS
    for j in reversed(range(ITERS)):
        partial = target[j]
        for k in range(j + 1, ITERS):
            partial = partial - matrix[j][k] * coeffs[k]
        coeffs[j] = partial / matrix[j][j]
    padded = jnp.concatenate(coeffs + [jnp.zeros((8 - ITERS, scenarios), jnp.float32)], axis=0)
    padded = jnp.concatenate([padded, jnp.zeros((8, 128 - scenarios), jnp.float32)], axis=1)
    columns = jnp.transpose(padded)[:scenarios]
    result = columns[:, 0:1] * fields_ref[0]
    for j in range(1, ITERS):
        result = result + columns[:, j : j + 1] * fields_ref[j]
    out_ref[...] = result
    safe_ref[0] = jnp.min(safe)


def gather_blocks(own):
    size = CHIPS * CORES
    pairs = [[CORES * chip + core for core in range(CORES)] for chip in range(CHIPS)]
    ring = [(i, (i + (CORES if i % CORES == 0 else -CORES)) % size) for i in range(size)]
    swap = [(i, i ^ 1) for i in range(size)]
    piece = lax.all_gather(own, "row", axis_index_groups=pairs)
    pieces = [piece]
    for distance in range(1, CHIPS // 2 + 1):
        piece = lax.ppermute(piece, "row", ring)
        pieces.append(piece)
        if distance < CHIPS // 2:
            pieces.append(lax.ppermute(piece, "row", swap))
    return pieces


def neighbours(field):
    size = lax.axis_size("row")
    up = [(i, i + 1) for i in range(size - 1)]
    down = [(j, i) for i, j in up]
    return lax.ppermute(field, "row", up), lax.ppermute(field, "row", down)


def near_apply(field, near_f32, link_gain):
    lower, upper = neighbours(field)
    result = field + jnp.dot(field, near_f32[1], precision=PRECISE)
    result = result + link_gain[0] * jnp.dot(lower, near_f32[0], precision=PRECISE)
    return result + link_gain[1] * jnp.dot(upper, near_f32[2], precision=PRECISE)


def jacobi_apply(field, jacobi_f32):
    return field + jnp.dot(field, jacobi_f32, precision=PRECISE)


def givens_solve(hessen, start_norm):
    matrix = [[hessen[i][k] for k in range(ITERS)] for i in range(ITERS + 1)]
    target = [start_norm] + [jnp.zeros_like(start_norm) for k in range(ITERS)]
    for j in range(ITERS):
        diag_val = matrix[j][j]
        below_val = matrix[j + 1][j]
        radius = jnp.sqrt(diag_val * diag_val + below_val * below_val)
        cosine = diag_val / radius
        sine_val = below_val / radius
        for k in range(j, ITERS):
            upper_val = matrix[j][k]
            lower_val = matrix[j + 1][k]
            matrix[j][k] = cosine * upper_val + sine_val * lower_val
            matrix[j + 1][k] = cosine * lower_val - sine_val * upper_val
        target[j + 1] = -sine_val * target[j]
        target[j] = cosine * target[j]
    coeffs = [None] * ITERS
    for j in reversed(range(ITERS)):
        partial_val = target[j]
        for k in range(j + 1, ITERS):
            partial_val = partial_val - matrix[j][k] * coeffs[k]
        coeffs[j] = partial_val / matrix[j][j]
    return coeffs


def stepwise_solve(initial, near, jacobi, link):
    near_f32 = near.astype(jnp.float32)
    jacobi_f32 = jacobi.astype(jnp.float32)
    link_gain = link.astype(jnp.float32)
    start_norm = jnp.sqrt(lax.psum(jnp.sum(initial * initial, axis=1), ("tile", "row")))
    basis = [initial / start_norm[:, None]]
    zero_row = jnp.zeros_like(start_norm)
    hessen = [[zero_row for k in range(ITERS)] for i in range(ITERS + 1)]
    for j in range(ITERS):
        candidate = jacobi_apply(near_apply(basis[j], near_f32, link_gain), jacobi_f32)
        local_dots = jnp.stack([jnp.sum(v * candidate, axis=1) for v in basis])
        projections = lax.psum(local_dots, ("tile", "row"))
        for i in range(j + 1):
            candidate = candidate - projections[i][:, None] * basis[i]
        new_norm = jnp.sqrt(lax.psum(jnp.sum(candidate * candidate, axis=1), ("tile", "row")))
        for i in range(j + 1):
            hessen[i][j] = projections[i]
        hessen[j + 1][j] = new_norm
        basis.append(candidate / new_norm[:, None])
    coeffs = givens_solve(hessen, start_norm)
    result = coeffs[0][:, None] * basis[0]
    for j in range(1, ITERS):
        result = result + coeffs[j][:, None] * basis[j]
    return result


def per_device(
    voltage, history, far_blocks, far_target, far_delay, near_blocks, near_link, jacobi_blocks
):
    voltage = voltage[0, 0, 0]
    history = history[0, 0]
    far_blocks = far_blocks[0, 0]
    targets = far_target[0, 0, :, 0]
    delays = far_delay[0, 0]
    near = near_blocks[0, 0]
    link = near_link[0, 0]
    jacobi = jacobi_blocks[0, 0]
    tiles, rows = lax.axis_size("tile"), lax.axis_size("row")
    scenarios, segments = voltage.shape
    f32 = jnp.float32
    field_shape = jax.ShapeDtypeStruct((scenarios, segments), f32)

    inputs = (targets, delays, link, near, jacobi, voltage, history, far_blocks)
    spaces = [pltpu.SMEM] * 3 + [pltpu.VMEM] * 5
    bucket, own_blocks, jacobi_kept = call(
        front_kernel,
        (
            jax.ShapeDtypeStruct((tiles, scenarios, segments), f32),
            jax.ShapeDtypeStruct(near.shape, f32),
            jax.ShapeDtypeStruct(jacobi.shape, jacobi.dtype),
        ),
        "s" + "h" * len(inputs),
        scratch_shapes=[space(x.shape, x.dtype) for space, x in zip(spaces, inputs)]
        + [pltpu.SemaphoreType.DMA((len(inputs) - 1,)), pltpu.SemaphoreType.DMA((4,))],
    )(lax.axis_index("tile").astype(jnp.int32)[None], *inputs)
    received = lax.all_to_all(bucket, "tile", split_axis=0, concat_axis=0, tiled=True)
    pieces = gather_blocks(own_blocks)
    initial = call(start_kernel, field_shape, "vv")(received, jacobi_kept)
    starts = lax.all_gather(initial, "row")
    place = lax.axis_index("row").astype(jnp.int32)[None]
    gram, own = krylov_call(place, starts, pieces, tiles)
    by_tile = lax.all_to_all(gram, "tile", split_axis=0, concat_axis=0, tiled=True)
    result, safe = call(
        solve_kernel,
        (field_shape, jax.ShapeDtypeStruct((1,), f32)),
        "vv",
        out_specs=(pl.BlockSpec(memory_space=pltpu.VMEM), pl.BlockSpec(memory_space=pltpu.SMEM)),
    )(by_tile, own)
    result = lax.cond(
        safe[0] > 0.5,
        lambda: result,
        lambda: stepwise_solve(initial, near, jacobi, link),
    )
    return result[None, None, None]


def solution(mesh):
    return jax.shard_map(
        per_device,
        mesh=mesh,
        in_specs=(
            P("tile", "row", None, None, None),
            P("tile", "row", None, None, None),
            P("tile", "row", None, None, None),
            P("tile", "row", None, None),
            P("tile", "row", None),
            P("tile", "row", None, None, None),
            P("tile", "row", None),
            P("tile", "row", None, None),
        ),
        out_specs=P("tile", "row", None, None, None),
        check_vma=False,
    )
```

```python
import jax
import jax.numpy as jnp
from jax import lax
from jax.experimental import pallas as pl
from jax.experimental.pallas import tpu as pltpu
from jax.sharding import PartitionSpec as P

ITERS = 5
BASIS = ITERS + 1
PAIRS = [(i, j) for i in range(BASIS) for j in range(i, BASIS)]
PIVOT_SHARE = 0.02
VMEM_BYTES = 20 * 1024 * 1024
PRECISE = lax.Precision.HIGHEST
CORES = 2
CHIPS = 8


def call(kernel, out_shape, in_spaces, **kwargs):
    spaces = {"v": pltpu.VMEM, "s": pltpu.SMEM, "h": pltpu.HBM}
    run = pl.pallas_call(
        kernel,
        out_shape=out_shape,
        in_specs=[pl.BlockSpec(memory_space=spaces[c]) for c in in_spaces],
        compiler_params=pltpu.CompilerParams(vmem_limit_bytes=VMEM_BYTES),
        **kwargs,
    )

    def placed(*operands):
        return run(
            *(
                pltpu.with_memory_space_constraint(x, pltpu.HBM) if c == "h" else x
                for c, x in zip(in_spaces, operands)
            )
        )

    return placed


def split_dot(field, block):
    rows = field.shape[0]
    high = field.astype(jnp.bfloat16)
    low = (field - high.astype(jnp.float32)).astype(jnp.bfloat16)
    both = jnp.dot(jnp.concatenate([high, low], axis=0), block, preferred_element_type=jnp.float32)
    return both[:rows] + both[rows:]


def ring_steps():
    steps = [0]
    for distance in range(1, CHIPS // 2 + 1):
        steps += [distance] if distance == CHIPS // 2 else [distance, -distance]
    return steps


def copy_in(sources, targets, sems):
    copies = [pltpu.make_async_copy(a, b, sems.at[i]) for i, (a, b) in enumerate(zip(sources, targets))]
    for copy in copies:
        copy.start()
    return copies


def blocks_kernel(link_hbm, near_hbm, jacobi_hbm, own_ref, kept_ref, link_ref, near_ref, jacobi_ref, sems):
    for copy in copy_in((link_hbm, near_hbm, jacobi_hbm), (link_ref, near_ref, jacobi_ref), sems):
        copy.wait()
    jacobi = jacobi_ref[...]
    kept_ref[...] = jacobi
    for side, gate in enumerate((link_ref[0], 1, link_ref[1])):
        near = near_ref[side]
        product = jnp.dot(near, jacobi, preferred_element_type=jnp.float32)
        merged = near.astype(jnp.float32) + product
        own_ref[side] = merged + jacobi.astype(jnp.float32) if side == 1 else merged * gate.astype(jnp.float32)


def far_kernel(
    tile_ref, target_hbm, delay_hbm, voltage_hbm, history_hbm, blocks_hbm, bucket_ref,
    target_ref, delay_ref, voltage_ref, history_ref, blocks_ref, sems, block_sems,
):
    entries, chunks = blocks_ref.shape[0], block_sems.shape[0]
    step = entries // chunks
    copies = copy_in(
        (target_hbm, delay_hbm, voltage_hbm, history_hbm),
        (target_ref, delay_ref, voltage_ref, history_ref),
        sems,
    )
    slices = [pl.ds(c * step, step) for c in range(chunks)]
    slabs = copy_in([blocks_hbm.at[s] for s in slices], [blocks_ref.at[s] for s in slices], block_sems)
    bucket_ref[...] = jnp.zeros_like(bucket_ref)
    for copy in copies:
        copy.wait()
    bucket_ref[tile_ref[0]] = -voltage_ref[...]
    for c in range(chunks):
        slabs[c].wait()
        for entry in range(c * step, (c + 1) * step):
            target = target_ref[entry]
            product = jnp.dot(
                history_ref[delay_ref[entry] - 1],
                blocks_ref[entry],
                preferred_element_type=jnp.float32,
            )
            bucket_ref[target] = bucket_ref[target] + product


def start_kernel(received_ref, jacobi_ref, out_ref):
    right_side = -jnp.sum(received_ref[...], axis=0)
    out_ref[...] = right_side + split_dot(right_side, jacobi_ref[...])


def krylov_kernel(place_ref, start_ref, *refs):
    chips = CHIPS
    piece_refs = refs[:chips]
    gram_ref, own_ref, fields, parts, highs, lows, sums = refs[chips:]
    rows, scenarios, segments = start_ref.shape
    cores = rows // chips
    zero_part = jnp.zeros(parts.shape[2:], parts.dtype)
    for side in range(2):
        parts[side, 0] = zero_part
        parts[side, rows + 1] = zero_part

    def halves(value):
        high = value.astype(jnp.bfloat16)
        low = (value - high.astype(jnp.float32)).astype(jnp.bfloat16)
        return high, low

    chip, core = lax.div(place_ref[0], cores), lax.rem(place_ref[0], cores)
    for piece_ref, steps in zip(piece_refs, ring_steps()):
        source = lax.rem(chip + (2 * core - 1) * steps + chips, chips)
        for core_there in range(cores):
            b = source * cores + core_there
            highs[b], lows[b] = halves(piece_ref[core_there].reshape(highs.shape[1:]))
    for b in range(rows):
        fields[0, b] = start_ref[b]
        parts[0, b + 1] = jnp.concatenate(halves(start_ref[b]), axis=0)

    for k in range(ITERS):
        now, later = k % 2, (k + 1) % 2
        for b in range(rows):
            around = jnp.concatenate([parts[now, b], parts[now, b + 1], parts[now, b + 2]], axis=1)
            main = jnp.dot(around, highs[b], preferred_element_type=jnp.float32)
            rest = jnp.dot(around[:scenarios], lows[b], preferred_element_type=jnp.float32)
            value = main[:scenarios] + (main[scenarios:] + rest)
            fields[k + 1, b] = value
            if k + 1 < ITERS:
                parts[later, b + 1] = jnp.concatenate(halves(value), axis=0)

    def gram(c, carry):
        at = pl.ds(pl.multiple_of(c * 8, 8), 8)
        totals = [jnp.zeros((8, segments), jnp.float32) for _ in PAIRS]
        for b in range(rows):
            values = [fields[i, b, at] for i in range(BASIS)]
            totals = [t + values[i] * values[j] for t, (i, j) in zip(totals, PAIRS)]
        for p, t in enumerate(totals):
            sums[p, at] = t
        return carry

    lax.fori_loop(0, scenarios // 8, gram, 0)
    for p in range(len(PAIRS), sums.shape[0]):
        sums[p] = jnp.zeros((scenarios, segments), jnp.float32)
    total = lax.dot_general(
        jnp.ones((8, segments), jnp.float32),
        sums[...].reshape(sums.shape[0] * scenarios, segments),
        (((1,), (1,)), ((), ())),
        precision=PRECISE,
        preferred_element_type=jnp.float32,
    )
    gram_ref[...] = jnp.broadcast_to(total[0:1][None], gram_ref.shape)
    for j in range(ITERS):
        own_ref[j] = fields[j, place_ref[0]]


def krylov_call(place, starts, pieces, tiles=32):
    rows, scenarios, segments = starts.shape
    f32 = jnp.float32
    padded_pairs = -(-len(PAIRS) * scenarios // 128) * 128 // scenarios
    return call(
        krylov_kernel,
        (
            jax.ShapeDtypeStruct((tiles, 1, padded_pairs * scenarios), f32),
            jax.ShapeDtypeStruct((ITERS, scenarios, segments), f32),
        ),
        "sv" + "v" * len(pieces),
        scratch_shapes=[
            pltpu.VMEM((BASIS, rows, scenarios, segments), f32),
            pltpu.VMEM((2, rows + 2, 2 * scenarios, segments), jnp.bfloat16),
            pltpu.VMEM((rows, 3 * segments, segments), jnp.bfloat16),
            pltpu.VMEM((rows, 3 * segments, segments), jnp.bfloat16),
            pltpu.VMEM((padded_pairs, scenarios, segments), f32),
        ],
    )(place, starts, *pieces)


def solve_kernel(received_ref, fields_ref, out_ref, safe_ref):
    total = jnp.sum(received_ref[...], axis=0)
    scenarios = out_ref.shape[0]
    gram = {pair: total[:, p * scenarios : (p + 1) * scenarios] for p, pair in enumerate(PAIRS)}
    factor = {}
    safe = jnp.ones((1, scenarios), jnp.float32)
    for i in range(BASIS):
        pivot = gram[i, i]
        for k in range(i):
            pivot = pivot - factor[k, i] * factor[k, i]
        safe = jnp.where(pivot >= PIVOT_SHARE * gram[i, i], safe, 0.0)
        safe = jnp.where(pivot > 0.0, safe, 0.0)
        safe = jnp.where(gram[i, i] < jnp.inf, safe, 0.0)
        factor[i, i] = jnp.sqrt(pivot)
        for j in range(i + 1, BASIS):
            entry = gram[i, j]
            for k in range(i):
                entry = entry - factor[k, i] * factor[k, j]
            factor[i, j] = entry / factor[i, i]
    matrix = [[None] * ITERS for _ in range(BASIS)]
    for j in range(ITERS):
        for i in range(j + 1):
            matrix[i][j] = factor[i, j] + factor[i, j + 1]
        matrix[j + 1][j] = factor[j + 1, j + 1]
    target = [factor[0, 0]] + [None] * ITERS
    for j in range(ITERS):
        diagonal, below = matrix[j][j], matrix[j + 1][j]
        radius = jnp.sqrt(diagonal * diagonal + below * below)
        cosine, sine = diagonal / radius, below / radius
        matrix[j][j] = radius
        for k in range(j + 1, ITERS):
            upper, lower = matrix[j][k], matrix[j + 1][k]
            matrix[j][k] = cosine * upper + sine * lower
            matrix[j + 1][k] = cosine * lower - sine * upper
        target[j + 1] = -sine * target[j]
        target[j] = cosine * target[j]
    coeffs = [None] * ITERS
    for j in reversed(range(ITERS)):
        partial = target[j]
        for k in range(j + 1, ITERS):
            partial = partial - matrix[j][k] * coeffs[k]
        coeffs[j] = partial / matrix[j][j]
    padded = jnp.concatenate(coeffs + [jnp.zeros((8 - ITERS, scenarios), jnp.float32)], axis=0)
    padded = jnp.concatenate([padded, jnp.zeros((8, 128 - scenarios), jnp.float32)], axis=1)
    columns = jnp.transpose(padded)[:scenarios]
    result = columns[:, 0:1] * fields_ref[0]
    for j in range(1, ITERS):
        result = result + columns[:, j : j + 1] * fields_ref[j]
    out_ref[...] = result
    safe_ref[0] = jnp.min(safe)


def gather_blocks(piece):
    size = CHIPS * CORES
    ring = [(i, (i + (CORES if i % CORES == 0 else -CORES)) % size) for i in range(size)]
    swap = [(i, i ^ 1) for i in range(size)]
    pieces = [piece]
    for distance in range(1, CHIPS // 2 + 1):
        piece = lax.ppermute(piece, "row", ring)
        pieces.append(piece)
        if distance < CHIPS // 2:
            pieces.append(lax.ppermute(piece, "row", swap))
    return pieces


def neighbours(field):
    size = lax.axis_size("row")
    up = [(i, i + 1) for i in range(size - 1)]
    down = [(j, i) for i, j in up]
    return lax.ppermute(field, "row", up), lax.ppermute(field, "row", down)


def near_apply(field, near_f32, link_gain):
    lower, upper = neighbours(field)
    result = field + jnp.dot(field, near_f32[1], precision=PRECISE)
    result = result + link_gain[0] * jnp.dot(lower, near_f32[0], precision=PRECISE)
    return result + link_gain[1] * jnp.dot(upper, near_f32[2], precision=PRECISE)


def jacobi_apply(field, jacobi_f32):
    return field + jnp.dot(field, jacobi_f32, precision=PRECISE)


def givens_solve(hessen, start_norm):
    matrix = [[hessen[i][k] for k in range(ITERS)] for i in range(ITERS + 1)]
    target = [start_norm] + [jnp.zeros_like(start_norm) for k in range(ITERS)]
    for j in range(ITERS):
        diag_val = matrix[j][j]
        below_val = matrix[j + 1][j]
        radius = jnp.sqrt(diag_val * diag_val + below_val * below_val)
        cosine = diag_val / radius
        sine_val = below_val / radius
        for k in range(j, ITERS):
            upper_val = matrix[j][k]
            lower_val = matrix[j + 1][k]
            matrix[j][k] = cosine * upper_val + sine_val * lower_val
            matrix[j + 1][k] = cosine * lower_val - sine_val * upper_val
        target[j + 1] = -sine_val * target[j]
        target[j] = cosine * target[j]
    coeffs = [None] * ITERS
    for j in reversed(range(ITERS)):
        partial_val = target[j]
        for k in range(j + 1, ITERS):
            partial_val = partial_val - matrix[j][k] * coeffs[k]
        coeffs[j] = partial_val / matrix[j][j]
    return coeffs


def stepwise_solve(initial, near, jacobi, link):
    near_f32 = near.astype(jnp.float32)
    jacobi_f32 = jacobi.astype(jnp.float32)
    link_gain = link.astype(jnp.float32)
    start_norm = jnp.sqrt(lax.psum(jnp.sum(initial * initial, axis=1), ("tile", "row")))
    basis = [initial / start_norm[:, None]]
    zero_row = jnp.zeros_like(start_norm)
    hessen = [[zero_row for k in range(ITERS)] for i in range(ITERS + 1)]
    for j in range(ITERS):
        candidate = jacobi_apply(near_apply(basis[j], near_f32, link_gain), jacobi_f32)
        local_dots = jnp.stack([jnp.sum(v * candidate, axis=1) for v in basis])
        projections = lax.psum(local_dots, ("tile", "row"))
        for i in range(j + 1):
            candidate = candidate - projections[i][:, None] * basis[i]
        new_norm = jnp.sqrt(lax.psum(jnp.sum(candidate * candidate, axis=1), ("tile", "row")))
        for i in range(j + 1):
            hessen[i][j] = projections[i]
        hessen[j + 1][j] = new_norm
        basis.append(candidate / new_norm[:, None])
    coeffs = givens_solve(hessen, start_norm)
    result = coeffs[0][:, None] * basis[0]
    for j in range(1, ITERS):
        result = result + coeffs[j][:, None] * basis[j]
    return result


def per_device(
    voltage, history, far_blocks, far_target, far_delay, near_blocks, near_link, jacobi_blocks
):
    voltage = voltage[0, 0, 0]
    history = history[0, 0]
    far_blocks = far_blocks[0, 0]
    targets = far_target[0, 0, :, 0]
    delays = far_delay[0, 0]
    near = near_blocks[0, 0]
    link = near_link[0, 0]
    jacobi = jacobi_blocks[0, 0]
    tiles, rows = lax.axis_size("tile"), lax.axis_size("row")
    scenarios, segments = voltage.shape
    f32 = jnp.float32
    field_shape = jax.ShapeDtypeStruct((scenarios, segments), f32)

    block_inputs = (link, near, jacobi)
    own_blocks, jacobi_kept = call(
        blocks_kernel,
        (jax.ShapeDtypeStruct(near.shape, f32), jax.ShapeDtypeStruct(jacobi.shape, jacobi.dtype)),
        "hhh",
        scratch_shapes=[
            space(x.shape, x.dtype) for space, x in zip((pltpu.SMEM, pltpu.VMEM, pltpu.VMEM), block_inputs)
        ]
        + [pltpu.SemaphoreType.DMA((len(block_inputs),))],
    )(*block_inputs)
    pairs = [[CORES * chip + core for core in range(CORES)] for chip in range(CHIPS)]
    piece = lax.all_gather(own_blocks, "row", axis_index_groups=pairs)
    pieces = gather_blocks(piece)
    targets, _ = lax.optimization_barrier((targets, piece))
    inputs = (targets, delays, voltage, history, far_blocks)
    spaces = [pltpu.SMEM] * 2 + [pltpu.VMEM] * 3
    bucket = call(
        far_kernel,
        jax.ShapeDtypeStruct((tiles, scenarios, segments), f32),
        "s" + "h" * len(inputs),
        scratch_shapes=[space(x.shape, x.dtype) for space, x in zip(spaces, inputs)]
        + [pltpu.SemaphoreType.DMA((len(inputs) - 1,)), pltpu.SemaphoreType.DMA((4,))],
    )(lax.axis_index("tile").astype(jnp.int32)[None], *inputs)
    bucket, _ = lax.optimization_barrier((bucket, pieces[1]))
    received = lax.all_to_all(bucket, "tile", split_axis=0, concat_axis=0, tiled=True)
    initial = call(start_kernel, field_shape, "vv")(received, jacobi_kept)
    starts = lax.all_gather(initial, "row")
    place = lax.axis_index("row").astype(jnp.int32)[None]
    gram, own = krylov_call(place, starts, pieces, tiles)
    by_tile = lax.all_to_all(gram, "tile", split_axis=0, concat_axis=0, tiled=True)
    result, safe = call(
        solve_kernel,
        (field_shape, jax.ShapeDtypeStruct((1,), f32)),
        "vv",
        out_specs=(pl.BlockSpec(memory_space=pltpu.VMEM), pl.BlockSpec(memory_space=pltpu.SMEM)),
    )(by_tile, own)
    safe, result = lax.while_loop(
        lambda state: state[0][0] < 0.5,
        lambda state: (jnp.ones_like(state[0]), stepwise_solve(initial, near, jacobi, link)),
        (safe, result),
    )
    return result[None, None, None]


def solution(mesh):
    return jax.shard_map(
        per_device,
        mesh=mesh,
        in_specs=(
            P("tile", "row", None, None, None),
            P("tile", "row", None, None, None),
            P("tile", "row", None, None, None),
            P("tile", "row", None, None),
            P("tile", "row", None),
            P("tile", "row", None, None, None),
            P("tile", "row", None),
            P("tile", "row", None, None),
        ),
        out_specs=P("tile", "row", None, None, None),
        check_vma=False,
    )
```

```python
import jax
import jax.numpy as jnp
from jax import lax
from jax.experimental import pallas as pl
from jax.experimental.pallas import tpu as pltpu
from jax.sharding import PartitionSpec as P

ITERS = 5
BASIS = ITERS + 1
PAIRS = [(i, j) for i in range(BASIS) for j in range(i, BASIS)]
PIVOT_SHARE = 0.02
VMEM_BYTES = 20 * 1024 * 1024
PRECISE = lax.Precision.HIGHEST
CORES = 2
CHIPS = 8
REACH = -(-(ITERS - 1) // CORES)


def call(kernel, out_shape, in_spaces, **kwargs):
    spaces = {"v": pltpu.VMEM, "s": pltpu.SMEM, "h": pltpu.HBM}
    run = pl.pallas_call(
        kernel,
        out_shape=out_shape,
        in_specs=[pl.BlockSpec(memory_space=spaces[c]) for c in in_spaces],
        compiler_params=pltpu.CompilerParams(vmem_limit_bytes=VMEM_BYTES),
        **kwargs,
    )

    def placed(*operands):
        return run(
            *(
                pltpu.with_memory_space_constraint(x, pltpu.HBM) if c == "h" else x
                for c, x in zip(in_spaces, operands)
            )
        )

    return placed


def split_dot(field, block):
    rows = field.shape[0]
    high = field.astype(jnp.bfloat16)
    low = (field - high.astype(jnp.float32)).astype(jnp.bfloat16)
    both = jnp.dot(jnp.concatenate([high, low], axis=0), block, preferred_element_type=jnp.float32)
    return both[:rows] + both[rows:]


def ring_steps():
    steps = [0]
    for distance in range(1, REACH + 1):
        steps += [distance, -distance]
    return steps


def front_kernel(
    tile_ref, target_hbm, delay_hbm, link_hbm, near_hbm, jacobi_hbm, voltage_hbm, history_hbm, blocks_hbm,
    bucket_ref, own_ref, kept_ref,
    target_ref, delay_ref, link_ref, near_ref, jacobi_ref, voltage_ref, history_ref, blocks_ref, sems, block_sems,
):
    entries, chunks = blocks_ref.shape[0], block_sems.shape[0]
    step = entries // chunks
    pairs = [
        (target_hbm, target_ref), (delay_hbm, delay_ref), (link_hbm, link_ref),
        (near_hbm, near_ref), (jacobi_hbm, jacobi_ref), (voltage_hbm, voltage_ref),
        (history_hbm, history_ref),
    ]
    copies = [pltpu.make_async_copy(a, b, sems.at[i]) for i, (a, b) in enumerate(pairs)]
    slabs = [
        pltpu.make_async_copy(
            blocks_hbm.at[pl.ds(c * step, step)], blocks_ref.at[pl.ds(c * step, step)], block_sems.at[c]
        )
        for c in range(chunks)
    ]
    for copy in copies + slabs:
        copy.start()
    bucket_ref[...] = jnp.zeros_like(bucket_ref)
    for copy in copies:
        copy.wait()
    jacobi = jacobi_ref[...]
    kept_ref[...] = jacobi
    for side, gate in enumerate((link_ref[0], 1, link_ref[1])):
        near = near_ref[side]
        product = jnp.dot(near, jacobi, preferred_element_type=jnp.float32)
        merged = near.astype(jnp.float32) + product
        own_ref[side] = merged + jacobi.astype(jnp.float32) if side == 1 else merged * gate.astype(jnp.float32)
    bucket_ref[tile_ref[0]] = -voltage_ref[...]
    for c in range(chunks):
        slabs[c].wait()
        for entry in range(c * step, (c + 1) * step):
            target = target_ref[entry]
            product = jnp.dot(
                history_ref[delay_ref[entry] - 1],
                blocks_ref[entry],
                preferred_element_type=jnp.float32,
            )
            bucket_ref[target] = bucket_ref[target] + product


def start_kernel(received_ref, jacobi_ref, out_ref):
    right_side = -jnp.sum(received_ref[...], axis=0)
    out_ref[...] = right_side + split_dot(right_side, jacobi_ref[...])


def krylov_kernel(place_ref, start_ref, *refs):
    steps = ring_steps()
    piece_refs = refs[: len(steps)]
    gram_ref, own_ref, fields, parts, highs, lows, sums = refs[len(steps) :]
    rows, scenarios, segments = start_ref.shape
    place = place_ref[0]
    core = lax.rem(place, CORES)
    middle = ITERS

    def halves(value):
        high = value.astype(jnp.bfloat16)
        low = (value - high.astype(jnp.float32)).astype(jnp.bfloat16)
        return high, low

    def inside(tile):
        return jnp.where((tile >= 0) & (tile < rows), 1.0, 0.0)

    for piece_ref, step in zip(piece_refs, steps):
        for there in range(CORES):
            away = (2 * core - 1) * (step * CORES) + there - core
            block = piece_ref[there].reshape(highs.shape[1:]) * inside(place + away)
            highs[away + middle], lows[away + middle] = halves(block)
    for away in range(-middle, middle + 1):
        tile = place + away
        field = start_ref[jnp.clip(tile, 0, rows - 1)] * inside(tile)
        parts[0, away + middle] = jnp.concatenate(halves(field), axis=0)
        if away == 0:
            fields[0] = field

    for k in range(ITERS):
        reach = ITERS - 1 - k
        for t in range(middle - reach, middle + reach + 1):
            around = jnp.concatenate([parts[k, t - 1], parts[k, t], parts[k, t + 1]], axis=1)
            main = jnp.dot(around, highs[t], preferred_element_type=jnp.float32)
            rest = jnp.dot(around[:scenarios], lows[t], preferred_element_type=jnp.float32)
            value = main[:scenarios] + (main[scenarios:] + rest)
            if t == middle:
                fields[k + 1] = value
            if k + 1 < ITERS:
                parts[k + 1, t] = jnp.concatenate(halves(value), axis=0)

    values = [fields[i] for i in range(BASIS)]
    for p, (i, j) in enumerate(PAIRS):
        sums[p] = values[i] * values[j]
    for p in range(len(PAIRS), sums.shape[0]):
        sums[p] = jnp.zeros((scenarios, segments), jnp.float32)
    total = lax.dot_general(
        jnp.ones((8, segments), jnp.float32),
        sums[...].reshape(sums.shape[0] * scenarios, segments),
        (((1,), (1,)), ((), ())),
        precision=PRECISE,
        preferred_element_type=jnp.float32,
    )
    gram_ref[...] = jnp.broadcast_to(total[0:1][None], gram_ref.shape)
    for j in range(ITERS):
        own_ref[j] = fields[j]


def krylov_call(place, starts, pieces):
    rows, scenarios, segments = starts.shape
    f32, bf16 = jnp.float32, jnp.bfloat16
    padded_pairs = -(-len(PAIRS) * scenarios // 128) * 128 // scenarios
    span = 2 * ITERS + 1
    return call(
        krylov_kernel,
        (
            jax.ShapeDtypeStruct((rows, 1, padded_pairs * scenarios), f32),
            jax.ShapeDtypeStruct((ITERS, scenarios, segments), f32),
        ),
        "sv" + "v" * len(pieces),
        scratch_shapes=[
            pltpu.VMEM((BASIS, scenarios, segments), f32),
            pltpu.VMEM((ITERS, span, 2 * scenarios, segments), bf16),
            pltpu.VMEM((span, 3 * segments, segments), bf16),
            pltpu.VMEM((span, 3 * segments, segments), bf16),
            pltpu.VMEM((padded_pairs, scenarios, segments), f32),
        ],
    )(place, starts, *pieces)


def add_kernel(received_ref, out_ref):
    total = jnp.sum(received_ref[...], axis=0)
    out_ref[...] = jnp.broadcast_to(total[None], out_ref.shape)


def solve_kernel(received_ref, fields_ref, out_ref, safe_ref):
    total = jnp.sum(received_ref[...], axis=0)
    scenarios = out_ref.shape[0]
    gram = {pair: total[:, p * scenarios : (p + 1) * scenarios] for p, pair in enumerate(PAIRS)}
    factor = {}
    safe = jnp.ones((1, scenarios), jnp.float32)
    for i in range(BASIS):
        pivot = gram[i, i]
        for k in range(i):
            pivot = pivot - factor[k, i] * factor[k, i]
        safe = jnp.where(pivot >= PIVOT_SHARE * gram[i, i], safe, 0.0)
        safe = jnp.where(pivot > 0.0, safe, 0.0)
        safe = jnp.where(gram[i, i] < jnp.inf, safe, 0.0)
        factor[i, i] = jnp.sqrt(pivot)
        for j in range(i + 1, BASIS):
            entry = gram[i, j]
            for k in range(i):
                entry = entry - factor[k, i] * factor[k, j]
            factor[i, j] = entry / factor[i, i]
    matrix = [[None] * ITERS for _ in range(BASIS)]
    for j in range(ITERS):
        for i in range(j + 1):
            matrix[i][j] = factor[i, j] + factor[i, j + 1]
        matrix[j + 1][j] = factor[j + 1, j + 1]
    target = [factor[0, 0]] + [None] * ITERS
    for j in range(ITERS):
        diagonal, below = matrix[j][j], matrix[j + 1][j]
        radius = jnp.sqrt(diagonal * diagonal + below * below)
        cosine, sine = diagonal / radius, below / radius
        matrix[j][j] = radius
        for k in range(j + 1, ITERS):
            upper, lower = matrix[j][k], matrix[j + 1][k]
            matrix[j][k] = cosine * upper + sine * lower
            matrix[j + 1][k] = cosine * lower - sine * upper
        target[j + 1] = -sine * target[j]
        target[j] = cosine * target[j]
    coeffs = [None] * ITERS
    for j in reversed(range(ITERS)):
        partial = target[j]
        for k in range(j + 1, ITERS):
            partial = partial - matrix[j][k] * coeffs[k]
        coeffs[j] = partial / matrix[j][j]
    padded = jnp.concatenate(coeffs + [jnp.zeros((8 - ITERS, scenarios), jnp.float32)], axis=0)
    padded = jnp.concatenate([padded, jnp.zeros((8, 128 - scenarios), jnp.float32)], axis=1)
    columns = jnp.transpose(padded)[:scenarios]
    result = columns[:, 0:1] * fields_ref[0]
    for j in range(1, ITERS):
        result = result + columns[:, j : j + 1] * fields_ref[j]
    out_ref[...] = result
    safe_ref[0] = jnp.min(safe)


def gather_blocks(own):
    size = CHIPS * CORES
    pairs = [[CORES * chip + core for core in range(CORES)] for chip in range(CHIPS)]
    ring = [(i, (i + (CORES if i % CORES == 0 else -CORES)) % size) for i in range(size)]
    swap = [(i, i ^ 1) for i in range(size)]
    piece = lax.all_gather(own, "row", axis_index_groups=pairs)
    pieces = [piece]
    for _ in range(REACH):
        piece = lax.ppermute(piece, "row", ring)
        given, _ = lax.optimization_barrier((piece, pieces[-1]))
        pieces += [piece, lax.ppermute(given, "row", swap)]
    return pieces


def neighbours(field):
    size = lax.axis_size("row")
    up = [(i, i + 1) for i in range(size - 1)]
    down = [(j, i) for i, j in up]
    return lax.ppermute(field, "row", up), lax.ppermute(field, "row", down)


def near_apply(field, near_f32, link_gain):
    lower, upper = neighbours(field)
    result = field + jnp.dot(field, near_f32[1], precision=PRECISE)
    result = result + link_gain[0] * jnp.dot(lower, near_f32[0], precision=PRECISE)
    return result + link_gain[1] * jnp.dot(upper, near_f32[2], precision=PRECISE)


def jacobi_apply(field, jacobi_f32):
    return field + jnp.dot(field, jacobi_f32, precision=PRECISE)


def givens_solve(hessen, start_norm):
    matrix = [[hessen[i][k] for k in range(ITERS)] for i in range(ITERS + 1)]
    target = [start_norm] + [jnp.zeros_like(start_norm) for k in range(ITERS)]
    for j in range(ITERS):
        diag_val = matrix[j][j]
        below_val = matrix[j + 1][j]
        radius = jnp.sqrt(diag_val * diag_val + below_val * below_val)
        cosine = diag_val / radius
        sine_val = below_val / radius
        for k in range(j, ITERS):
            upper_val = matrix[j][k]
            lower_val = matrix[j + 1][k]
            matrix[j][k] = cosine * upper_val + sine_val * lower_val
            matrix[j + 1][k] = cosine * lower_val - sine_val * upper_val
        target[j + 1] = -sine_val * target[j]
        target[j] = cosine * target[j]
    coeffs = [None] * ITERS
    for j in reversed(range(ITERS)):
        partial_val = target[j]
        for k in range(j + 1, ITERS):
            partial_val = partial_val - matrix[j][k] * coeffs[k]
        coeffs[j] = partial_val / matrix[j][j]
    return coeffs


def stepwise_solve(initial, near, jacobi, link):
    near_f32 = near.astype(jnp.float32)
    jacobi_f32 = jacobi.astype(jnp.float32)
    link_gain = link.astype(jnp.float32)
    start_norm = jnp.sqrt(lax.psum(jnp.sum(initial * initial, axis=1), ("tile", "row")))
    basis = [initial / start_norm[:, None]]
    zero_row = jnp.zeros_like(start_norm)
    hessen = [[zero_row for k in range(ITERS)] for i in range(ITERS + 1)]
    for j in range(ITERS):
        candidate = jacobi_apply(near_apply(basis[j], near_f32, link_gain), jacobi_f32)
        local_dots = jnp.stack([jnp.sum(v * candidate, axis=1) for v in basis])
        projections = lax.psum(local_dots, ("tile", "row"))
        for i in range(j + 1):
            candidate = candidate - projections[i][:, None] * basis[i]
        new_norm = jnp.sqrt(lax.psum(jnp.sum(candidate * candidate, axis=1), ("tile", "row")))
        for i in range(j + 1):
            hessen[i][j] = projections[i]
        hessen[j + 1][j] = new_norm
        basis.append(candidate / new_norm[:, None])
    coeffs = givens_solve(hessen, start_norm)
    result = coeffs[0][:, None] * basis[0]
    for j in range(1, ITERS):
        result = result + coeffs[j][:, None] * basis[j]
    return result


def per_device(
    voltage, history, far_blocks, far_target, far_delay, near_blocks, near_link, jacobi_blocks
):
    voltage = voltage[0, 0, 0]
    history = history[0, 0]
    far_blocks = far_blocks[0, 0]
    targets = far_target[0, 0, :, 0]
    delays = far_delay[0, 0]
    near = near_blocks[0, 0]
    link = near_link[0, 0]
    jacobi = jacobi_blocks[0, 0]
    tiles, rows = lax.axis_size("tile"), lax.axis_size("row")
    scenarios, segments = voltage.shape
    f32 = jnp.float32
    field_shape = jax.ShapeDtypeStruct((scenarios, segments), f32)

    inputs = (targets, delays, link, near, jacobi, voltage, history, far_blocks)
    spaces = [pltpu.SMEM] * 3 + [pltpu.VMEM] * 5
    bucket, own_blocks, jacobi_kept = call(
        front_kernel,
        (
            jax.ShapeDtypeStruct((tiles, scenarios, segments), f32),
            jax.ShapeDtypeStruct(near.shape, f32),
            jax.ShapeDtypeStruct(jacobi.shape, jacobi.dtype),
        ),
        "s" + "h" * len(inputs),
        scratch_shapes=[space(x.shape, x.dtype) for space, x in zip(spaces, inputs)]
        + [pltpu.SemaphoreType.DMA((len(inputs) - 1,)), pltpu.SemaphoreType.DMA((4,))],
    )(lax.axis_index("tile").astype(jnp.int32)[None], *inputs)
    received = lax.all_to_all(bucket, "tile", split_axis=0, concat_axis=0, tiled=True)
    pieces = gather_blocks(own_blocks)
    initial = call(start_kernel, field_shape, "vv")(received, jacobi_kept)
    starts = lax.all_gather(initial, "row")
    place = lax.axis_index("row").astype(jnp.int32)[None]
    gram, own = krylov_call(place, starts, pieces)
    by_row = lax.all_to_all(gram, "row", split_axis=0, concat_axis=0, tiled=True)
    group = call(add_kernel, jax.ShapeDtypeStruct((tiles,) + gram.shape[1:], f32), "v")(by_row)
    by_tile = lax.all_to_all(group, "tile", split_axis=0, concat_axis=0, tiled=True)
    result, safe = call(
        solve_kernel,
        (field_shape, jax.ShapeDtypeStruct((1,), f32)),
        "vv",
        out_specs=(pl.BlockSpec(memory_space=pltpu.VMEM), pl.BlockSpec(memory_space=pltpu.SMEM)),
    )(by_tile, own)
    safe, result = lax.while_loop(
        lambda state: state[0][0] < 0.5,
        lambda state: (jnp.ones_like(state[0]), stepwise_solve(initial, near, jacobi, link)),
        (safe, result),
    )
    return result[None, None, None]


def solution(mesh):
    return jax.shard_map(
        per_device,
        mesh=mesh,
        in_specs=(
            P("tile", "row", None, None, None),
            P("tile", "row", None, None, None),
            P("tile", "row", None, None, None),
            P("tile", "row", None, None),
            P("tile", "row", None),
            P("tile", "row", None, None, None),
            P("tile", "row", None),
            P("tile", "row", None, None),
        ),
        out_specs=P("tile", "row", None, None, None),
        check_vma=False,
    )
```

```python
import jax
import jax.numpy as jnp
from jax import lax
from jax.experimental import pallas as pl
from jax.experimental.pallas import tpu as pltpu
from jax.sharding import PartitionSpec as P

ITERS = 5
BASIS = ITERS + 1
PAIRS = [(i, j) for i in range(BASIS) for j in range(i, BASIS)]
PIVOT_SHARE = 0.02
VMEM_BYTES = 20 * 1024 * 1024
PRECISE = lax.Precision.HIGHEST
CORES = 2
CHIPS = 8
REACH = -(-(ITERS - 1) // CORES)


def call(kernel, out_shape, in_spaces, **kwargs):
    spaces = {"v": pltpu.VMEM, "s": pltpu.SMEM, "h": pltpu.HBM}
    run = pl.pallas_call(
        kernel,
        out_shape=out_shape,
        in_specs=[pl.BlockSpec(memory_space=spaces[c]) for c in in_spaces],
        compiler_params=pltpu.CompilerParams(vmem_limit_bytes=VMEM_BYTES),
        **kwargs,
    )

    def placed(*operands):
        return run(
            *(
                pltpu.with_memory_space_constraint(x, pltpu.HBM) if c == "h" else x
                for c, x in zip(in_spaces, operands)
            )
        )

    return placed


def split_dot(field, block):
    rows = field.shape[0]
    high = field.astype(jnp.bfloat16)
    low = (field - high.astype(jnp.float32)).astype(jnp.bfloat16)
    both = jnp.dot(jnp.concatenate([high, low], axis=0), block, preferred_element_type=jnp.float32)
    return both[:rows] + both[rows:]


def ring_steps():
    return list(range(REACH + 1)) + [-distance for distance in range(1, REACH + 1)]


def front_kernel(
    tile_ref, target_hbm, delay_hbm, link_hbm, near_hbm, jacobi_hbm, voltage_hbm, history_hbm, blocks_hbm,
    bucket_ref, own_ref, kept_ref, gates_ref,
    target_ref, delay_ref, link_ref, near_ref, jacobi_ref, voltage_ref, history_ref, blocks_ref, sems, block_sems,
):
    entries, chunks = blocks_ref.shape[0], block_sems.shape[0]
    step = entries // chunks
    pairs = [
        (target_hbm, target_ref), (delay_hbm, delay_ref), (link_hbm, link_ref),
        (near_hbm, near_ref), (jacobi_hbm, jacobi_ref), (voltage_hbm, voltage_ref),
        (history_hbm, history_ref),
    ]
    copies = [pltpu.make_async_copy(a, b, sems.at[i]) for i, (a, b) in enumerate(pairs)]
    slabs = [
        pltpu.make_async_copy(
            blocks_hbm.at[pl.ds(c * step, step)], blocks_ref.at[pl.ds(c * step, step)], block_sems.at[c]
        )
        for c in range(chunks)
    ]
    for copy in copies + slabs:
        copy.start()
    bucket_ref[...] = jnp.zeros_like(bucket_ref)
    for copy in copies:
        copy.wait()
    jacobi = jacobi_ref[...]
    kept_ref[...] = jacobi
    for side in range(2):
        gates_ref[side : side + 1] = jnp.full((1, gates_ref.shape[1]), link_ref[side].astype(jnp.float32))
    for side, gate in enumerate((link_ref[0], 1, link_ref[1])):
        near = near_ref[side]
        product = jnp.dot(near, jacobi, preferred_element_type=jnp.float32)
        merged = near.astype(jnp.float32) + product
        own_ref[side] = merged + jacobi.astype(jnp.float32) if side == 1 else merged * gate.astype(jnp.float32)
    bucket_ref[tile_ref[0]] = -voltage_ref[...]
    for c in range(chunks):
        slabs[c].wait()
        for entry in range(c * step, (c + 1) * step):
            target = target_ref[entry]
            product = jnp.dot(
                history_ref[delay_ref[entry] - 1],
                blocks_ref[entry],
                preferred_element_type=jnp.float32,
            )
            bucket_ref[target] = bucket_ref[target] + product


def front_call(tile, inputs, tiles):
    near, jacobi, voltage = inputs[3:6]
    f32 = jnp.float32
    spaces = [pltpu.SMEM] * 3 + [pltpu.VMEM] * 5
    return call(
        front_kernel,
        (
            jax.ShapeDtypeStruct((tiles,) + voltage.shape, f32),
            jax.ShapeDtypeStruct(near.shape, f32),
            jax.ShapeDtypeStruct(jacobi.shape, jacobi.dtype),
            jax.ShapeDtypeStruct((2, jacobi.shape[0]), f32),
        ),
        "s" + "h" * len(inputs),
        scratch_shapes=[space(x.shape, x.dtype) for space, x in zip(spaces, inputs)]
        + [pltpu.SemaphoreType.DMA((len(inputs) - 1,)), pltpu.SemaphoreType.DMA((4,))],
    )(tile, *inputs)


def start_kernel(received_ref, jacobi_ref, out_ref):
    right_side = -jnp.sum(received_ref[...], axis=0)
    out_ref[...] = right_side + split_dot(right_side, jacobi_ref[...])


def krylov_kernel(place_ref, start_ref, *refs):
    steps = ring_steps()
    given_ref = refs[REACH + 1]
    piece_refs = list(refs[: REACH + 1]) + [given_ref.at[i] for i in range(REACH)]
    gram_ref, own_ref, fields, parts, highs, lows, sums = refs[REACH + 2 :]
    rows, scenarios, segments = start_ref.shape
    place = place_ref[0]
    core = lax.rem(place, CORES)
    middle = ITERS

    def halves(value):
        high = value.astype(jnp.bfloat16)
        low = (value - high.astype(jnp.float32)).astype(jnp.bfloat16)
        return high, low

    def inside(tile):
        return jnp.where((tile >= 0) & (tile < rows), 1.0, 0.0)

    for piece_ref, step in zip(piece_refs, steps):
        for there in range(CORES):
            away = (2 * core - 1) * (step * CORES) + there - core
            block = piece_ref[there].reshape(highs.shape[1:]) * inside(place + away)
            highs[away + middle], lows[away + middle] = halves(block)
    for away in range(-middle, middle + 1):
        tile = place + away
        field = start_ref[jnp.clip(tile, 0, rows - 1)] * inside(tile)
        parts[0, away + middle] = jnp.concatenate(halves(field), axis=0)
        if away == 0:
            fields[0] = field

    for k in range(ITERS):
        reach = ITERS - 1 - k
        for t in range(middle - reach, middle + reach + 1):
            around = jnp.concatenate([parts[k, t - 1], parts[k, t], parts[k, t + 1]], axis=1)
            main = jnp.dot(around, highs[t], preferred_element_type=jnp.float32)
            rest = jnp.dot(around[:scenarios], lows[t], preferred_element_type=jnp.float32)
            value = main[:scenarios] + (main[scenarios:] + rest)
            if t == middle:
                fields[k + 1] = value
            if k + 1 < ITERS:
                parts[k + 1, t] = jnp.concatenate(halves(value), axis=0)

    values = [fields[i] for i in range(BASIS)]
    for p, (i, j) in enumerate(PAIRS):
        sums[p] = values[i] * values[j]
    for p in range(len(PAIRS), sums.shape[0]):
        sums[p] = jnp.zeros((scenarios, segments), jnp.float32)
    total = lax.dot_general(
        jnp.ones((8, segments), jnp.float32),
        sums[...].reshape(sums.shape[0] * scenarios, segments),
        (((1,), (1,)), ((), ())),
        precision=PRECISE,
        preferred_element_type=jnp.float32,
    )
    gram_ref[...] = jnp.broadcast_to(total[0:1][None], gram_ref.shape)
    for j in range(ITERS):
        own_ref[j] = fields[j]


def krylov_call(place, starts, pieces):
    rows, scenarios, segments = starts.shape
    f32, bf16 = jnp.float32, jnp.bfloat16
    padded_pairs = -(-len(PAIRS) * scenarios // 128) * 128 // scenarios
    span = 2 * ITERS + 1
    return call(
        krylov_kernel,
        (
            jax.ShapeDtypeStruct((rows, 1, padded_pairs * scenarios), f32),
            jax.ShapeDtypeStruct((ITERS, scenarios, segments), f32),
        ),
        "sv" + "v" * len(pieces),
        scratch_shapes=[
            pltpu.VMEM((BASIS, scenarios, segments), f32),
            pltpu.VMEM((ITERS, span, 2 * scenarios, segments), bf16),
            pltpu.VMEM((span, 3 * segments, segments), bf16),
            pltpu.VMEM((span, 3 * segments, segments), bf16),
            pltpu.VMEM((padded_pairs, scenarios, segments), f32),
        ],
    )(place, starts, *pieces)


def add_kernel(received_ref, out_ref):
    total = jnp.sum(received_ref[...], axis=0)
    out_ref[...] = jnp.broadcast_to(total[None], out_ref.shape)


def solve_kernel(received_ref, fields_ref, out_ref, safe_ref):
    total = jnp.sum(received_ref[...], axis=0)
    scenarios = out_ref.shape[0]
    gram = {pair: total[:, p * scenarios : (p + 1) * scenarios] for p, pair in enumerate(PAIRS)}
    factor = {}
    safe = jnp.ones((1, scenarios), jnp.float32)
    for i in range(BASIS):
        pivot = gram[i, i]
        for k in range(i):
            pivot = pivot - factor[k, i] * factor[k, i]
        safe = jnp.where(pivot >= PIVOT_SHARE * gram[i, i], safe, 0.0)
        safe = jnp.where(pivot > 0.0, safe, 0.0)
        safe = jnp.where(gram[i, i] < jnp.inf, safe, 0.0)
        factor[i, i] = jnp.sqrt(pivot)
        for j in range(i + 1, BASIS):
            entry = gram[i, j]
            for k in range(i):
                entry = entry - factor[k, i] * factor[k, j]
            factor[i, j] = entry / factor[i, i]
    matrix = [[None] * ITERS for _ in range(BASIS)]
    for j in range(ITERS):
        for i in range(j + 1):
            matrix[i][j] = factor[i, j] + factor[i, j + 1]
        matrix[j + 1][j] = factor[j + 1, j + 1]
    target = [factor[0, 0]] + [None] * ITERS
    for j in range(ITERS):
        diagonal, below = matrix[j][j], matrix[j + 1][j]
        radius = jnp.sqrt(diagonal * diagonal + below * below)
        cosine, sine = diagonal / radius, below / radius
        matrix[j][j] = radius
        for k in range(j + 1, ITERS):
            upper, lower = matrix[j][k], matrix[j + 1][k]
            matrix[j][k] = cosine * upper + sine * lower
            matrix[j + 1][k] = cosine * lower - sine * upper
        target[j + 1] = -sine * target[j]
        target[j] = cosine * target[j]
    coeffs = [None] * ITERS
    for j in reversed(range(ITERS)):
        partial = target[j]
        for k in range(j + 1, ITERS):
            partial = partial - matrix[j][k] * coeffs[k]
        coeffs[j] = partial / matrix[j][j]
    padded = jnp.concatenate(coeffs + [jnp.zeros((8 - ITERS, scenarios), jnp.float32)], axis=0)
    padded = jnp.concatenate([padded, jnp.zeros((8, 128 - scenarios), jnp.float32)], axis=1)
    columns = jnp.transpose(padded)[:scenarios]
    result = columns[:, 0:1] * fields_ref[0]
    for j in range(1, ITERS):
        result = result + columns[:, j : j + 1] * fields_ref[j]
    out_ref[...] = result
    safe_ref[0] = jnp.min(safe)


def gather_blocks(own):
    size = CHIPS * CORES
    pairs = [[CORES * chip + core for core in range(CORES)] for chip in range(CHIPS)]
    ring = [(i, (i + (CORES if i % CORES == 0 else -CORES)) % size) for i in range(size)]
    swap = [(i, i ^ 1) for i in range(size)]
    piece = lax.all_gather(own, "row", axis_index_groups=pairs)
    pieces = [piece]
    for _ in range(REACH):
        piece = lax.ppermute(piece, "row", ring)
        pieces.append(piece)
    return pieces + [lax.ppermute(jnp.stack(pieces[1:]), "row", swap)]


def neighbours(field):
    size = lax.axis_size("row")
    up = [(i, i + 1) for i in range(size - 1)]
    down = [(j, i) for i, j in up]
    return lax.ppermute(field, "row", up), lax.ppermute(field, "row", down)


def near_apply(field, near_f32, link_gain):
    lower, upper = neighbours(field)
    result = field + jnp.dot(field, near_f32[1], precision=PRECISE)
    result = result + link_gain[0] * jnp.dot(lower, near_f32[0], precision=PRECISE)
    return result + link_gain[1] * jnp.dot(upper, near_f32[2], precision=PRECISE)


def jacobi_apply(field, jacobi_f32):
    return field + jnp.dot(field, jacobi_f32, precision=PRECISE)


def givens_solve(hessen, start_norm):
    matrix = [[hessen[i][k] for k in range(ITERS)] for i in range(ITERS + 1)]
    target = [start_norm] + [jnp.zeros_like(start_norm) for k in range(ITERS)]
    for j in range(ITERS):
        diag_val = matrix[j][j]
        below_val = matrix[j + 1][j]
        radius = jnp.sqrt(diag_val * diag_val + below_val * below_val)
        cosine = diag_val / radius
        sine_val = below_val / radius
        for k in range(j, ITERS):
            upper_val = matrix[j][k]
            lower_val = matrix[j + 1][k]
            matrix[j][k] = cosine * upper_val + sine_val * lower_val
            matrix[j + 1][k] = cosine * lower_val - sine_val * upper_val
        target[j + 1] = -sine_val * target[j]
        target[j] = cosine * target[j]
    coeffs = [None] * ITERS
    for j in reversed(range(ITERS)):
        partial_val = target[j]
        for k in range(j + 1, ITERS):
            partial_val = partial_val - matrix[j][k] * coeffs[k]
        coeffs[j] = partial_val / matrix[j][j]
    return coeffs


def stepwise_solve(initial, near, jacobi, link_gain):
    near_f32 = near.astype(jnp.float32)
    jacobi_f32 = jacobi.astype(jnp.float32)
    start_norm = jnp.sqrt(lax.psum(jnp.sum(initial * initial, axis=1), ("tile", "row")))
    basis = [initial / start_norm[:, None]]
    zero_row = jnp.zeros_like(start_norm)
    hessen = [[zero_row for k in range(ITERS)] for i in range(ITERS + 1)]
    for j in range(ITERS):
        candidate = jacobi_apply(near_apply(basis[j], near_f32, link_gain), jacobi_f32)
        local_dots = jnp.stack([jnp.sum(v * candidate, axis=1) for v in basis])
        projections = lax.psum(local_dots, ("tile", "row"))
        for i in range(j + 1):
            candidate = candidate - projections[i][:, None] * basis[i]
        new_norm = jnp.sqrt(lax.psum(jnp.sum(candidate * candidate, axis=1), ("tile", "row")))
        for i in range(j + 1):
            hessen[i][j] = projections[i]
        hessen[j + 1][j] = new_norm
        basis.append(candidate / new_norm[:, None])
    coeffs = givens_solve(hessen, start_norm)
    result = coeffs[0][:, None] * basis[0]
    for j in range(1, ITERS):
        result = result + coeffs[j][:, None] * basis[j]
    return result


def per_device(
    voltage, history, far_blocks, far_target, far_delay, near_blocks, near_link, jacobi_blocks
):
    voltage = voltage[0, 0, 0]
    history = history[0, 0]
    far_blocks = far_blocks[0, 0]
    targets = far_target[0, 0, :, 0]
    delays = far_delay[0, 0]
    near = near_blocks[0, 0]
    link = near_link[0, 0]
    jacobi = jacobi_blocks[0, 0]
    tiles, rows = lax.axis_size("tile"), lax.axis_size("row")
    scenarios, segments = voltage.shape
    f32 = jnp.float32
    field_shape = jax.ShapeDtypeStruct((scenarios, segments), f32)

    tile = lax.axis_index("tile").astype(jnp.int32)[None]
    bucket, own_blocks, jacobi_kept, gates = front_call(
        tile, (targets, delays, link, near, jacobi, voltage, history, far_blocks), tiles
    )
    received = lax.all_to_all(bucket, "tile", split_axis=0, concat_axis=0, tiled=True)
    pieces = gather_blocks(own_blocks)
    initial = call(start_kernel, field_shape, "vv")(received, jacobi_kept)
    starts = lax.all_gather(initial, "row")
    place = lax.axis_index("row").astype(jnp.int32)[None]
    gram, own = krylov_call(place, starts, pieces)
    by_row = lax.all_to_all(gram, "row", split_axis=0, concat_axis=0, tiled=True)
    group = call(add_kernel, jax.ShapeDtypeStruct((tiles,) + gram.shape[1:], f32), "v")(by_row)
    by_tile = lax.all_to_all(group, "tile", split_axis=0, concat_axis=0, tiled=True)
    result, safe = call(
        solve_kernel,
        (field_shape, jax.ShapeDtypeStruct((1,), f32)),
        "vv",
        out_specs=(pl.BlockSpec(memory_space=pltpu.VMEM), pl.BlockSpec(memory_space=pltpu.SMEM)),
    )(by_tile, own)
    safe, result = lax.while_loop(
        lambda state: state[0][0] < 0.5,
        lambda state: (jnp.ones_like(state[0]), stepwise_solve(initial, near, jacobi_kept, gates)),
        (safe, result),
    )
    return result[None, None, None]


def solution(mesh):
    return jax.shard_map(
        per_device,
        mesh=mesh,
        in_specs=(
            P("tile", "row", None, None, None),
            P("tile", "row", None, None, None),
            P("tile", "row", None, None, None),
            P("tile", "row", None, None),
            P("tile", "row", None),
            P("tile", "row", None, None, None),
            P("tile", "row", None),
            P("tile", "row", None, None),
        ),
        out_specs=P("tile", "row", None, None, None),
        check_vma=False,
    )
```

```python
import jax
import jax.numpy as jnp
from jax import lax
from jax.experimental import pallas as pl
from jax.experimental.pallas import tpu as pltpu
from jax.sharding import PartitionSpec as P

ITERS = 5
BASIS = ITERS + 1
PAIRS = [(i, j) for i in range(BASIS) for j in range(i, BASIS)]
PIVOT_SHARE = 0.02
VMEM_BYTES = 20 * 1024 * 1024
PRECISE = lax.Precision.HIGHEST
CORES = 2
CHIPS = 8
REACH = -(-(ITERS - 1) // CORES)


def call(kernel, out_shape, in_spaces, **kwargs):
    spaces = {"v": pltpu.VMEM, "s": pltpu.SMEM, "h": pltpu.HBM}
    run = pl.pallas_call(
        kernel,
        out_shape=out_shape,
        in_specs=[pl.BlockSpec(memory_space=spaces[c]) for c in in_spaces],
        compiler_params=pltpu.CompilerParams(vmem_limit_bytes=VMEM_BYTES),
        **kwargs,
    )

    def placed(*operands):
        return run(
            *(
                pltpu.with_memory_space_constraint(x, pltpu.HBM) if c == "h" else x
                for c, x in zip(in_spaces, operands)
            )
        )

    return placed


def split_dot(field, block):
    rows = field.shape[0]
    high = field.astype(jnp.bfloat16)
    low = (field - high.astype(jnp.float32)).astype(jnp.bfloat16)
    both = jnp.dot(jnp.concatenate([high, low], axis=0), block, preferred_element_type=jnp.float32)
    return both[:rows] + both[rows:]


def ring_steps():
    return list(range(REACH + 1)) + [-distance for distance in range(1, REACH + 1)]


def front_kernel(
    tile_ref, target_hbm, delay_hbm, link_hbm, near_hbm, jacobi_hbm, voltage_hbm, history_hbm, blocks_hbm,
    bucket_ref, own_ref, kept_ref, gates_ref,
    target_ref, delay_ref, link_ref, near_ref, jacobi_ref, voltage_ref, history_ref, blocks_ref, sems, block_sems,
):
    entries, chunks = blocks_ref.shape[0], block_sems.shape[0]
    step = entries // chunks
    pairs = [
        (target_hbm, target_ref), (delay_hbm, delay_ref), (link_hbm, link_ref),
        (near_hbm, near_ref), (jacobi_hbm, jacobi_ref), (voltage_hbm, voltage_ref),
        (history_hbm, history_ref),
    ]
    copies = [pltpu.make_async_copy(a, b, sems.at[i]) for i, (a, b) in enumerate(pairs)]
    slabs = [
        pltpu.make_async_copy(
            blocks_hbm.at[pl.ds(c * step, step)], blocks_ref.at[pl.ds(c * step, step)], block_sems.at[c]
        )
        for c in range(chunks)
    ]
    for copy in copies + slabs:
        copy.start()
    bucket_ref[...] = jnp.zeros_like(bucket_ref)
    for copy in copies:
        copy.wait()
    jacobi = jacobi_ref[...]
    kept_ref[...] = jacobi
    for side in range(2):
        gates_ref[side : side + 1] = jnp.full((1, gates_ref.shape[1]), link_ref[side].astype(jnp.float32))
    for side, gate in enumerate((link_ref[0], 1, link_ref[1])):
        near = near_ref[side]
        product = jnp.dot(near, jacobi, preferred_element_type=jnp.float32)
        merged = near.astype(jnp.float32) + product
        own_ref[side] = merged + jacobi.astype(jnp.float32) if side == 1 else merged * gate.astype(jnp.float32)
    bucket_ref[tile_ref[0]] = -voltage_ref[...]
    for c in range(chunks):
        slabs[c].wait()
        for entry in range(c * step, (c + 1) * step):
            target = target_ref[entry]
            product = jnp.dot(
                history_ref[delay_ref[entry] - 1],
                blocks_ref[entry],
                preferred_element_type=jnp.float32,
            )
            bucket_ref[target] = bucket_ref[target] + product


def front_call(tile, inputs, tiles):
    near, jacobi, voltage = inputs[3:6]
    f32 = jnp.float32
    spaces = [pltpu.SMEM] * 3 + [pltpu.VMEM] * 5
    return call(
        front_kernel,
        (
            jax.ShapeDtypeStruct((tiles,) + voltage.shape, f32),
            jax.ShapeDtypeStruct(near.shape, f32),
            jax.ShapeDtypeStruct(jacobi.shape, jacobi.dtype),
            jax.ShapeDtypeStruct((2, jacobi.shape[0]), f32),
        ),
        "s" + "h" * len(inputs),
        scratch_shapes=[space(x.shape, x.dtype) for space, x in zip(spaces, inputs)]
        + [pltpu.SemaphoreType.DMA((len(inputs) - 1,)), pltpu.SemaphoreType.DMA((4,))],
    )(tile, *inputs)


def start_kernel(received_ref, jacobi_ref, out_ref):
    right_side = -jnp.sum(received_ref[...], axis=0)
    out_ref[...] = right_side + split_dot(right_side, jacobi_ref[...])


def krylov_kernel(place_ref, start_ref, *refs):
    steps = ring_steps()
    given_ref = refs[REACH + 1]
    piece_refs = list(refs[: REACH + 1]) + [given_ref.at[i] for i in range(REACH)]
    gram_ref, own_ref, fields, parts, highs, lows, sums = refs[REACH + 2 :]
    rows, scenarios, segments = start_ref.shape
    place = place_ref[0]
    core = lax.rem(place, CORES)
    middle = ITERS

    def halves(value):
        high = value.astype(jnp.bfloat16)
        low = (value - high.astype(jnp.float32)).astype(jnp.bfloat16)
        return high, low

    def inside(tile):
        return jnp.where((tile >= 0) & (tile < rows), 1.0, 0.0)

    for piece_ref, step in zip(piece_refs, steps):
        for there in range(CORES):
            away = (2 * core - 1) * (step * CORES) + there - core
            block = piece_ref[there].reshape(highs.shape[1:]) * inside(place + away)
            highs[away + middle], lows[away + middle] = halves(block)
    for away in range(-middle, middle + 1):
        tile = place + away
        field = start_ref[jnp.clip(tile, 0, rows - 1)] * inside(tile)
        parts[0, away + middle] = jnp.concatenate(halves(field), axis=0)
        if away == 0:
            fields[0] = field

    for k in range(ITERS):
        reach = ITERS - 1 - k
        for t in range(middle - reach, middle + reach + 1):
            around = jnp.concatenate([parts[k, t - 1], parts[k, t], parts[k, t + 1]], axis=1)
            main = jnp.dot(around, highs[t], preferred_element_type=jnp.float32)
            rest = jnp.dot(around[:scenarios], lows[t], preferred_element_type=jnp.float32)
            value = main[:scenarios] + (main[scenarios:] + rest)
            if t == middle:
                fields[k + 1] = value
            if k + 1 < ITERS:
                parts[k + 1, t] = jnp.concatenate(halves(value), axis=0)

    values = [fields[i] for i in range(BASIS)]
    for p, (i, j) in enumerate(PAIRS):
        sums[p] = values[i] * values[j]
    for p in range(len(PAIRS), sums.shape[0]):
        sums[p] = jnp.zeros((scenarios, segments), jnp.float32)
    total = lax.dot_general(
        jnp.ones((8, segments), jnp.float32),
        sums[...].reshape(sums.shape[0] * scenarios, segments),
        (((1,), (1,)), ((), ())),
        precision=PRECISE,
        preferred_element_type=jnp.float32,
    )
    gram_ref[...] = jnp.broadcast_to(total[0:1][None], gram_ref.shape)
    for j in range(ITERS):
        own_ref[j] = fields[j]


def krylov_call(place, starts, pieces):
    rows, scenarios, segments = starts.shape
    f32, bf16 = jnp.float32, jnp.bfloat16
    padded_pairs = -(-len(PAIRS) * scenarios // 128) * 128 // scenarios
    span = 2 * ITERS + 1
    return call(
        krylov_kernel,
        (
            jax.ShapeDtypeStruct((rows, 1, padded_pairs * scenarios), f32),
            jax.ShapeDtypeStruct((ITERS, scenarios, segments), f32),
        ),
        "sv" + "v" * len(pieces),
        scratch_shapes=[
            pltpu.VMEM((BASIS, scenarios, segments), f32),
            pltpu.VMEM((ITERS, span, 2 * scenarios, segments), bf16),
            pltpu.VMEM((span, 3 * segments, segments), bf16),
            pltpu.VMEM((span, 3 * segments, segments), bf16),
            pltpu.VMEM((padded_pairs, scenarios, segments), f32),
        ],
    )(place, starts, *pieces)


def hand_on_kernel(fields_ref, out_ref):
    out_ref[...] = fields_ref[...]


def add_kernel(received_ref, out_ref):
    total = jnp.sum(received_ref[...], axis=0)
    out_ref[...] = jnp.broadcast_to(total[None], out_ref.shape)


def solve_kernel(received_ref, fields_ref, out_ref, safe_ref):
    total = jnp.sum(received_ref[...], axis=0)
    scenarios = out_ref.shape[0]
    gram = {pair: total[:, p * scenarios : (p + 1) * scenarios] for p, pair in enumerate(PAIRS)}
    factor = {}
    safe = jnp.ones((1, scenarios), jnp.float32)
    for i in range(BASIS):
        pivot = gram[i, i]
        for k in range(i):
            pivot = pivot - factor[k, i] * factor[k, i]
        safe = jnp.where(pivot >= PIVOT_SHARE * gram[i, i], safe, 0.0)
        safe = jnp.where(pivot > 0.0, safe, 0.0)
        safe = jnp.where(gram[i, i] < jnp.inf, safe, 0.0)
        factor[i, i] = jnp.sqrt(pivot)
        inverse = 1.0 / factor[i, i]
        for j in range(i + 1, BASIS):
            entry = gram[i, j]
            for k in range(i):
                entry = entry - factor[k, i] * factor[k, j]
            factor[i, j] = entry * inverse
    matrix = [[None] * ITERS for _ in range(BASIS)]
    for j in range(ITERS):
        for i in range(j + 1):
            matrix[i][j] = factor[i, j] + factor[i, j + 1]
        matrix[j + 1][j] = factor[j + 1, j + 1]
    target = [factor[0, 0]] + [None] * ITERS
    inverses = [None] * ITERS
    for j in range(ITERS):
        diagonal, below = matrix[j][j], matrix[j + 1][j]
        radius = jnp.sqrt(diagonal * diagonal + below * below)
        inverses[j] = 1.0 / radius
        cosine, sine = diagonal * inverses[j], below * inverses[j]
        for k in range(j + 1, ITERS):
            upper, lower = matrix[j][k], matrix[j + 1][k]
            matrix[j][k] = cosine * upper + sine * lower
            matrix[j + 1][k] = cosine * lower - sine * upper
        target[j + 1] = -sine * target[j]
        target[j] = cosine * target[j]
    coeffs = [None] * ITERS
    for j in reversed(range(ITERS)):
        partial = target[j]
        for k in range(j + 1, ITERS):
            partial = partial - matrix[j][k] * coeffs[k]
        coeffs[j] = partial * inverses[j]
    padded = jnp.concatenate(coeffs + [jnp.zeros((8 - ITERS, scenarios), jnp.float32)], axis=0)
    padded = jnp.concatenate([padded, jnp.zeros((8, 128 - scenarios), jnp.float32)], axis=1)
    columns = jnp.transpose(padded)[:scenarios]
    result = columns[:, 0:1] * fields_ref[0]
    for j in range(1, ITERS):
        result = result + columns[:, j : j + 1] * fields_ref[j]
    out_ref[...] = result
    safe_ref[0] = jnp.min(safe)


def gather_blocks(own):
    size = CHIPS * CORES
    pairs = [[CORES * chip + core for core in range(CORES)] for chip in range(CHIPS)]
    ring = [(i, (i + (CORES if i % CORES == 0 else -CORES)) % size) for i in range(size)]
    swap = [(i, i ^ 1) for i in range(size)]
    piece = lax.all_gather(own, "row", axis_index_groups=pairs)
    pieces = [piece]
    for _ in range(REACH):
        piece = lax.ppermute(piece, "row", ring)
        pieces.append(piece)
    return pieces + [lax.ppermute(jnp.stack(pieces[1:]), "row", swap)]


def neighbours(field):
    size = lax.axis_size("row")
    up = [(i, i + 1) for i in range(size - 1)]
    down = [(j, i) for i, j in up]
    return lax.ppermute(field, "row", up), lax.ppermute(field, "row", down)


def near_apply(field, near_f32, link_gain):
    lower, upper = neighbours(field)
    result = field + jnp.dot(field, near_f32[1], precision=PRECISE)
    result = result + link_gain[0] * jnp.dot(lower, near_f32[0], precision=PRECISE)
    return result + link_gain[1] * jnp.dot(upper, near_f32[2], precision=PRECISE)


def jacobi_apply(field, jacobi_f32):
    return field + jnp.dot(field, jacobi_f32, precision=PRECISE)


def givens_solve(hessen, start_norm):
    matrix = [[hessen[i][k] for k in range(ITERS)] for i in range(ITERS + 1)]
    target = [start_norm] + [jnp.zeros_like(start_norm) for k in range(ITERS)]
    for j in range(ITERS):
        diag_val = matrix[j][j]
        below_val = matrix[j + 1][j]
        radius = jnp.sqrt(diag_val * diag_val + below_val * below_val)
        cosine = diag_val / radius
        sine_val = below_val / radius
        for k in range(j, ITERS):
            upper_val = matrix[j][k]
            lower_val = matrix[j + 1][k]
            matrix[j][k] = cosine * upper_val + sine_val * lower_val
            matrix[j + 1][k] = cosine * lower_val - sine_val * upper_val
        target[j + 1] = -sine_val * target[j]
        target[j] = cosine * target[j]
    coeffs = [None] * ITERS
    for j in reversed(range(ITERS)):
        partial_val = target[j]
        for k in range(j + 1, ITERS):
            partial_val = partial_val - matrix[j][k] * coeffs[k]
        coeffs[j] = partial_val / matrix[j][j]
    return coeffs


def stepwise_solve(initial, near, jacobi, link_gain):
    near_f32 = near.astype(jnp.float32)
    jacobi_f32 = jacobi.astype(jnp.float32)
    start_norm = jnp.sqrt(lax.psum(jnp.sum(initial * initial, axis=1), ("tile", "row")))
    basis = [initial / start_norm[:, None]]
    zero_row = jnp.zeros_like(start_norm)
    hessen = [[zero_row for k in range(ITERS)] for i in range(ITERS + 1)]
    for j in range(ITERS):
        candidate = jacobi_apply(near_apply(basis[j], near_f32, link_gain), jacobi_f32)
        local_dots = jnp.stack([jnp.sum(v * candidate, axis=1) for v in basis])
        projections = lax.psum(local_dots, ("tile", "row"))
        for i in range(j + 1):
            candidate = candidate - projections[i][:, None] * basis[i]
        new_norm = jnp.sqrt(lax.psum(jnp.sum(candidate * candidate, axis=1), ("tile", "row")))
        for i in range(j + 1):
            hessen[i][j] = projections[i]
        hessen[j + 1][j] = new_norm
        basis.append(candidate / new_norm[:, None])
    coeffs = givens_solve(hessen, start_norm)
    result = coeffs[0][:, None] * basis[0]
    for j in range(1, ITERS):
        result = result + coeffs[j][:, None] * basis[j]
    return result


def per_device(
    voltage, history, far_blocks, far_target, far_delay, near_blocks, near_link, jacobi_blocks
):
    voltage = voltage[0, 0, 0]
    history = history[0, 0]
    far_blocks = far_blocks[0, 0]
    targets = far_target[0, 0, :, 0]
    delays = far_delay[0, 0]
    near = near_blocks[0, 0]
    link = near_link[0, 0]
    jacobi = jacobi_blocks[0, 0]
    tiles, rows = lax.axis_size("tile"), lax.axis_size("row")
    scenarios, segments = voltage.shape
    f32 = jnp.float32
    field_shape = jax.ShapeDtypeStruct((scenarios, segments), f32)

    tile = lax.axis_index("tile").astype(jnp.int32)[None]
    bucket, own_blocks, jacobi_kept, gates = front_call(
        tile, (targets, delays, link, near, jacobi, voltage, history, far_blocks), tiles
    )
    received = lax.all_to_all(bucket, "tile", split_axis=0, concat_axis=0, tiled=True)
    pieces = gather_blocks(own_blocks)
    initial = call(start_kernel, field_shape, "vv")(received, jacobi_kept)
    starts = lax.all_gather(initial, "row")
    place = lax.axis_index("row").astype(jnp.int32)[None]
    gram, own = krylov_call(place, starts, pieces)
    by_row = lax.all_to_all(gram, "row", split_axis=0, concat_axis=0, tiled=True)
    own = call(hand_on_kernel, jax.ShapeDtypeStruct(own.shape, f32), "v")(own)
    by_row, own = lax.optimization_barrier((by_row, own))
    group = call(add_kernel, jax.ShapeDtypeStruct((tiles,) + gram.shape[1:], f32), "v")(by_row)
    by_tile = lax.all_to_all(group, "tile", split_axis=0, concat_axis=0, tiled=True)
    own = call(hand_on_kernel, jax.ShapeDtypeStruct(own.shape, f32), "v")(own)
    result, safe = call(
        solve_kernel,
        (field_shape, jax.ShapeDtypeStruct((1,), f32)),
        "vv",
        out_specs=(pl.BlockSpec(memory_space=pltpu.VMEM), pl.BlockSpec(memory_space=pltpu.SMEM)),
    )(by_tile, own)
    safe, result = lax.while_loop(
        lambda state: state[0][0] < 0.5,
        lambda state: (jnp.ones_like(state[0]), stepwise_solve(initial, near, jacobi_kept, gates)),
        (safe, result),
    )
    return result[None, None, None]


def solution(mesh):
    return jax.shard_map(
        per_device,
        mesh=mesh,
        in_specs=(
            P("tile", "row", None, None, None),
            P("tile", "row", None, None, None),
            P("tile", "row", None, None, None),
            P("tile", "row", None, None),
            P("tile", "row", None),
            P("tile", "row", None, None, None),
            P("tile", "row", None),
            P("tile", "row", None, None),
        ),
        out_specs=P("tile", "row", None, None, None),
        check_vma=False,
    )
```

```python
import jax
import jax.numpy as jnp
from jax import lax
from jax.experimental import pallas as pl
from jax.experimental.pallas import tpu as pltpu
from jax.sharding import PartitionSpec as P

ITERS = 5
BASIS = ITERS + 1
PAIRS = [(i, j) for i in range(BASIS) for j in range(i, BASIS)]
PIVOT_SHARE = 0.02
VMEM_BYTES = 20 * 1024 * 1024
PRECISE = lax.Precision.HIGHEST
CORES = 2
CHIPS = 8
REACH = -(-(ITERS - 1) // CORES)


def call(kernel, out_shape, in_spaces, **kwargs):
    spaces = {"v": pltpu.VMEM, "s": pltpu.SMEM, "h": pltpu.HBM}
    run = pl.pallas_call(
        kernel,
        out_shape=out_shape,
        in_specs=[pl.BlockSpec(memory_space=spaces[c]) for c in in_spaces],
        compiler_params=pltpu.CompilerParams(vmem_limit_bytes=VMEM_BYTES),
        **kwargs,
    )

    def placed(*operands):
        return run(
            *(
                pltpu.with_memory_space_constraint(x, pltpu.HBM) if c == "h" else x
                for c, x in zip(in_spaces, operands)
            )
        )

    return placed


def split_dot(field, block):
    rows = field.shape[0]
    high = field.astype(jnp.bfloat16)
    low = (field - high.astype(jnp.float32)).astype(jnp.bfloat16)
    both = jnp.dot(jnp.concatenate([high, low], axis=0), block, preferred_element_type=jnp.float32)
    return both[:rows] + both[rows:]


def ring_steps():
    return list(range(REACH + 1)) + [-distance for distance in range(1, REACH + 1)]


def front_kernel(
    tile_ref, target_hbm, delay_hbm, link_hbm, near_hbm, jacobi_hbm, voltage_hbm, history_hbm, blocks_hbm,
    bucket_ref, own_ref, kept_ref, gates_ref,
    target_ref, delay_ref, link_ref, near_ref, jacobi_ref, voltage_ref, history_ref, blocks_ref, sems, block_sems,
):
    entries, chunks = blocks_ref.shape[0], block_sems.shape[0]
    step = entries // chunks
    pairs = [
        (target_hbm, target_ref), (delay_hbm, delay_ref), (link_hbm, link_ref),
        (near_hbm, near_ref), (jacobi_hbm, jacobi_ref), (voltage_hbm, voltage_ref),
        (history_hbm, history_ref),
    ]
    copies = [pltpu.make_async_copy(a, b, sems.at[i]) for i, (a, b) in enumerate(pairs)]
    slabs = [
        pltpu.make_async_copy(
            blocks_hbm.at[pl.ds(c * step, step)], blocks_ref.at[pl.ds(c * step, step)], block_sems.at[c]
        )
        for c in range(chunks)
    ]
    for copy in copies + slabs:
        copy.start()
    bucket_ref[...] = jnp.zeros_like(bucket_ref)
    for copy in copies:
        copy.wait()
    jacobi = jacobi_ref[...]
    kept_ref[...] = jacobi
    for side in range(2):
        gates_ref[side : side + 1] = jnp.full((1, gates_ref.shape[1]), link_ref[side].astype(jnp.float32))
    for side, gate in enumerate((link_ref[0], 1, link_ref[1])):
        near = near_ref[side]
        product = jnp.dot(near, jacobi, preferred_element_type=jnp.float32)
        merged = near.astype(jnp.float32) + product
        own_ref[side] = merged + jacobi.astype(jnp.float32) if side == 1 else merged * gate.astype(jnp.float32)
    bucket_ref[tile_ref[0]] = -voltage_ref[...]
    for c in range(chunks):
        slabs[c].wait()
        for entry in range(c * step, (c + 1) * step):
            target = target_ref[entry]
            product = jnp.dot(
                history_ref[delay_ref[entry] - 1],
                blocks_ref[entry],
                preferred_element_type=jnp.float32,
            )
            bucket_ref[target] = bucket_ref[target] + product


def front_call(tile, inputs, tiles):
    near, jacobi, voltage = inputs[3:6]
    f32 = jnp.float32
    spaces = [pltpu.SMEM] * 3 + [pltpu.VMEM] * 5
    return call(
        front_kernel,
        (
            jax.ShapeDtypeStruct((tiles,) + voltage.shape, f32),
            jax.ShapeDtypeStruct(near.shape, f32),
            jax.ShapeDtypeStruct(jacobi.shape, jacobi.dtype),
            jax.ShapeDtypeStruct((2, jacobi.shape[0]), f32),
        ),
        "s" + "h" * len(inputs),
        scratch_shapes=[space(x.shape, x.dtype) for space, x in zip(spaces, inputs)]
        + [pltpu.SemaphoreType.DMA((len(inputs) - 1,)), pltpu.SemaphoreType.DMA((1,))],
    )(tile, *inputs)


def start_kernel(received_ref, jacobi_ref, out_ref):
    right_side = -jnp.sum(received_ref[...], axis=0)
    out_ref[...] = right_side + split_dot(right_side, jacobi_ref[...])


def krylov_kernel(place_ref, start_ref, *refs):
    steps = ring_steps()
    given_ref = refs[REACH + 1]
    piece_refs = list(refs[: REACH + 1]) + [given_ref.at[i] for i in range(REACH)]
    gram_ref, own_ref, fields, parts, highs, lows, sums = refs[REACH + 2 :]
    rows, scenarios, segments = start_ref.shape
    place = place_ref[0]
    core = lax.rem(place, CORES)
    middle = ITERS

    def halves(value):
        high = value.astype(jnp.bfloat16)
        low = (value - high.astype(jnp.float32)).astype(jnp.bfloat16)
        return high, low

    def inside(tile):
        return jnp.where((tile >= 0) & (tile < rows), 1.0, 0.0)

    for piece_ref, step in zip(piece_refs, steps):
        for there in range(CORES):
            away = (2 * core - 1) * (step * CORES) + there - core
            block = piece_ref[there].reshape(highs.shape[1:]) * inside(place + away)
            highs[away + middle], lows[away + middle] = halves(block)
    for away in range(-middle, middle + 1):
        tile = place + away
        field = start_ref[jnp.clip(tile, 0, rows - 1)] * inside(tile)
        parts[0, away + middle] = jnp.concatenate(halves(field), axis=0)
        if away == 0:
            fields[0] = field

    for k in range(ITERS):
        reach = ITERS - 1 - k
        for t in range(middle - reach, middle + reach + 1):
            around = jnp.concatenate([parts[k, t - 1], parts[k, t], parts[k, t + 1]], axis=1)
            main = jnp.dot(around, highs[t], preferred_element_type=jnp.float32)
            rest = jnp.dot(around[:scenarios], lows[t], preferred_element_type=jnp.float32)
            value = main[:scenarios] + (main[scenarios:] + rest)
            if t == middle:
                fields[k + 1] = value
            if k + 1 < ITERS:
                parts[k + 1, t] = jnp.concatenate(halves(value), axis=0)

    values = [fields[i] for i in range(BASIS)]
    for p, (i, j) in enumerate(PAIRS):
        sums[p] = values[i] * values[j]
    for p in range(len(PAIRS), sums.shape[0]):
        sums[p] = jnp.zeros((scenarios, segments), jnp.float32)
    total = lax.dot_general(
        jnp.ones((8, segments), jnp.float32),
        sums[...].reshape(sums.shape[0] * scenarios, segments),
        (((1,), (1,)), ((), ())),
        precision=PRECISE,
        preferred_element_type=jnp.float32,
    )
    gram_ref[...] = jnp.broadcast_to(total[0:1][None], gram_ref.shape)
    for j in range(ITERS):
        own_ref[j] = fields[j]


def krylov_call(place, starts, pieces):
    rows, scenarios, segments = starts.shape
    f32, bf16 = jnp.float32, jnp.bfloat16
    padded_pairs = -(-len(PAIRS) * scenarios // 128) * 128 // scenarios
    span = 2 * ITERS + 1
    return call(
        krylov_kernel,
        (
            jax.ShapeDtypeStruct((rows, 1, padded_pairs * scenarios), f32),
            jax.ShapeDtypeStruct((ITERS, scenarios, segments), f32),
        ),
        "sv" + "v" * len(pieces),
        scratch_shapes=[
            pltpu.VMEM((BASIS, scenarios, segments), f32),
            pltpu.VMEM((ITERS, span, 2 * scenarios, segments), bf16),
            pltpu.VMEM((span, 3 * segments, segments), bf16),
            pltpu.VMEM((span, 3 * segments, segments), bf16),
            pltpu.VMEM((padded_pairs, scenarios, segments), f32),
        ],
    )(place, starts, *pieces)


def add_kernel(received_ref, out_ref):
    total = jnp.sum(received_ref[...], axis=0)
    out_ref[...] = jnp.broadcast_to(total[None], out_ref.shape)


def solve_kernel(received_ref, fields_ref, out_ref, safe_ref):
    total = jnp.sum(received_ref[...], axis=0)
    scenarios = out_ref.shape[0]
    gram = {pair: total[:, p * scenarios : (p + 1) * scenarios] for p, pair in enumerate(PAIRS)}
    factor = {}
    safe = jnp.ones((1, scenarios), jnp.float32)
    for i in range(BASIS):
        pivot = gram[i, i]
        for k in range(i):
            pivot = pivot - factor[k, i] * factor[k, i]
        safe = jnp.where(pivot >= PIVOT_SHARE * gram[i, i], safe, 0.0)
        safe = jnp.where(pivot > 0.0, safe, 0.0)
        safe = jnp.where(gram[i, i] < jnp.inf, safe, 0.0)
        factor[i, i] = jnp.sqrt(pivot)
        for j in range(i + 1, BASIS):
            entry = gram[i, j]
            for k in range(i):
                entry = entry - factor[k, i] * factor[k, j]
            factor[i, j] = entry / factor[i, i]
    matrix = [[None] * ITERS for _ in range(BASIS)]
    for j in range(ITERS):
        for i in range(j + 1):
            matrix[i][j] = factor[i, j] + factor[i, j + 1]
        matrix[j + 1][j] = factor[j + 1, j + 1]
    target = [factor[0, 0]] + [None] * ITERS
    for j in range(ITERS):
        diagonal, below = matrix[j][j], matrix[j + 1][j]
        radius = jnp.sqrt(diagonal * diagonal + below * below)
        cosine, sine = diagonal / radius, below / radius
        matrix[j][j] = radius
        for k in range(j + 1, ITERS):
            upper, lower = matrix[j][k], matrix[j + 1][k]
            matrix[j][k] = cosine * upper + sine * lower
            matrix[j + 1][k] = cosine * lower - sine * upper
        target[j + 1] = -sine * target[j]
        target[j] = cosine * target[j]
    coeffs = [None] * ITERS
    for j in reversed(range(ITERS)):
        partial = target[j]
        for k in range(j + 1, ITERS):
            partial = partial - matrix[j][k] * coeffs[k]
        coeffs[j] = partial / matrix[j][j]
    padded = jnp.concatenate(coeffs + [jnp.zeros((8 - ITERS, scenarios), jnp.float32)], axis=0)
    padded = jnp.concatenate([padded, jnp.zeros((8, 128 - scenarios), jnp.float32)], axis=1)
    columns = jnp.transpose(padded)[:scenarios]
    result = columns[:, 0:1] * fields_ref[0]
    for j in range(1, ITERS):
        result = result + columns[:, j : j + 1] * fields_ref[j]
    out_ref[...] = result
    safe_ref[0] = jnp.min(safe)


def gather_blocks(own):
    size = CHIPS * CORES
    pairs = [[CORES * chip + core for core in range(CORES)] for chip in range(CHIPS)]
    ring = [(i, (i + (CORES if i % CORES == 0 else -CORES)) % size) for i in range(size)]
    swap = [(i, i ^ 1) for i in range(size)]
    piece = lax.all_gather(own, "row", axis_index_groups=pairs)
    pieces = [piece]
    for _ in range(REACH):
        piece = lax.ppermute(piece, "row", ring)
        pieces.append(piece)
    return pieces + [lax.ppermute(jnp.stack(pieces[1:]), "row", swap)]


def neighbours(field):
    size = lax.axis_size("row")
    up = [(i, i + 1) for i in range(size - 1)]
    down = [(j, i) for i, j in up]
    return lax.ppermute(field, "row", up), lax.ppermute(field, "row", down)


def near_apply(field, near_f32, link_gain):
    lower, upper = neighbours(field)
    result = field + jnp.dot(field, near_f32[1], precision=PRECISE)
    result = result + link_gain[0] * jnp.dot(lower, near_f32[0], precision=PRECISE)
    return result + link_gain[1] * jnp.dot(upper, near_f32[2], precision=PRECISE)


def jacobi_apply(field, jacobi_f32):
    return field + jnp.dot(field, jacobi_f32, precision=PRECISE)


def givens_solve(hessen, start_norm):
    matrix = [[hessen[i][k] for k in range(ITERS)] for i in range(ITERS + 1)]
    target = [start_norm] + [jnp.zeros_like(start_norm) for k in range(ITERS)]
    for j in range(ITERS):
        diag_val = matrix[j][j]
        below_val = matrix[j + 1][j]
        radius = jnp.sqrt(diag_val * diag_val + below_val * below_val)
        cosine = diag_val / radius
        sine_val = below_val / radius
        for k in range(j, ITERS):
            upper_val = matrix[j][k]
            lower_val = matrix[j + 1][k]
            matrix[j][k] = cosine * upper_val + sine_val * lower_val
            matrix[j + 1][k] = cosine * lower_val - sine_val * upper_val
        target[j + 1] = -sine_val * target[j]
        target[j] = cosine * target[j]
    coeffs = [None] * ITERS
    for j in reversed(range(ITERS)):
        partial_val = target[j]
        for k in range(j + 1, ITERS):
            partial_val = partial_val - matrix[j][k] * coeffs[k]
        coeffs[j] = partial_val / matrix[j][j]
    return coeffs


def stepwise_solve(initial, near, jacobi, link_gain):
    near_f32 = near.astype(jnp.float32)
    jacobi_f32 = jacobi.astype(jnp.float32)
    start_norm = jnp.sqrt(lax.psum(jnp.sum(initial * initial, axis=1), ("tile", "row")))
    basis = [initial / start_norm[:, None]]
    zero_row = jnp.zeros_like(start_norm)
    hessen = [[zero_row for k in range(ITERS)] for i in range(ITERS + 1)]
    for j in range(ITERS):
        candidate = jacobi_apply(near_apply(basis[j], near_f32, link_gain), jacobi_f32)
        local_dots = jnp.stack([jnp.sum(v * candidate, axis=1) for v in basis])
        projections = lax.psum(local_dots, ("tile", "row"))
        for i in range(j + 1):
            candidate = candidate - projections[i][:, None] * basis[i]
        new_norm = jnp.sqrt(lax.psum(jnp.sum(candidate * candidate, axis=1), ("tile", "row")))
        for i in range(j + 1):
            hessen[i][j] = projections[i]
        hessen[j + 1][j] = new_norm
        basis.append(candidate / new_norm[:, None])
    coeffs = givens_solve(hessen, start_norm)
    result = coeffs[0][:, None] * basis[0]
    for j in range(1, ITERS):
        result = result + coeffs[j][:, None] * basis[j]
    return result


def per_device(
    voltage, history, far_blocks, far_target, far_delay, near_blocks, near_link, jacobi_blocks
):
    voltage = voltage[0, 0, 0]
    history = history[0, 0]
    far_blocks = far_blocks[0, 0]
    targets = far_target[0, 0, :, 0]
    delays = far_delay[0, 0]
    near = near_blocks[0, 0]
    link = near_link[0, 0]
    jacobi = jacobi_blocks[0, 0]
    tiles, rows = lax.axis_size("tile"), lax.axis_size("row")
    scenarios, segments = voltage.shape
    f32 = jnp.float32
    field_shape = jax.ShapeDtypeStruct((scenarios, segments), f32)

    tile = lax.axis_index("tile").astype(jnp.int32)[None]
    bucket, own_blocks, jacobi_kept, gates = front_call(
        tile, (targets, delays, link, near, jacobi, voltage, history, far_blocks), tiles
    )
    received = lax.all_to_all(bucket, "tile", split_axis=0, concat_axis=0, tiled=True)
    pieces = gather_blocks(own_blocks)
    initial = call(start_kernel, field_shape, "vv")(received, jacobi_kept)
    starts = lax.all_gather(initial, "row")
    place = lax.axis_index("row").astype(jnp.int32)[None]
    gram, own = krylov_call(place, starts, pieces)
    by_row = lax.all_to_all(gram, "row", split_axis=0, concat_axis=0, tiled=True)
    group = call(add_kernel, jax.ShapeDtypeStruct((tiles,) + gram.shape[1:], f32), "v")(by_row)
    by_tile = lax.all_to_all(group, "tile", split_axis=0, concat_axis=0, tiled=True)
    result, safe = call(
        solve_kernel,
        (field_shape, jax.ShapeDtypeStruct((1,), f32)),
        "vv",
        out_specs=(pl.BlockSpec(memory_space=pltpu.VMEM), pl.BlockSpec(memory_space=pltpu.SMEM)),
    )(by_tile, own)
    safe, result = lax.while_loop(
        lambda state: state[0][0] < 0.5,
        lambda state: (jnp.ones_like(state[0]), stepwise_solve(initial, near, jacobi_kept, gates)),
        (safe, result),
    )
    return result[None, None, None]


def solution(mesh):
    return jax.shard_map(
        per_device,
        mesh=mesh,
        in_specs=(
            P("tile", "row", None, None, None),
            P("tile", "row", None, None, None),
            P("tile", "row", None, None, None),
            P("tile", "row", None, None),
            P("tile", "row", None),
            P("tile", "row", None, None, None),
            P("tile", "row", None),
            P("tile", "row", None, None),
        ),
        out_specs=P("tile", "row", None, None, None),
        check_vma=False,
    )
```

```python
import jax
import jax.numpy as jnp
from jax import lax
from jax.experimental import pallas as pl
from jax.experimental.pallas import tpu as pltpu
from jax.sharding import PartitionSpec as P

ITERS = 5
BASIS = ITERS + 1
PAIRS = [(i, j) for i in range(BASIS) for j in range(i, BASIS)]
PIVOT_SHARE = 0.02
VMEM_BYTES = 20 * 1024 * 1024
PRECISE = lax.Precision.HIGHEST
CORES = 2
CHIPS = 8
REACH = -(-(ITERS - 1) // CORES)


def call(kernel, out_shape, in_spaces, **kwargs):
    spaces = {"v": pltpu.VMEM, "s": pltpu.SMEM, "h": pltpu.HBM}
    run = pl.pallas_call(
        kernel,
        out_shape=out_shape,
        in_specs=[pl.BlockSpec(memory_space=spaces[c]) for c in in_spaces],
        compiler_params=pltpu.CompilerParams(vmem_limit_bytes=VMEM_BYTES),
        **kwargs,
    )

    def placed(*operands):
        return run(
            *(
                pltpu.with_memory_space_constraint(x, pltpu.HBM) if c == "h" else x
                for c, x in zip(in_spaces, operands)
            )
        )

    return placed


def split_dot(field, block):
    rows = field.shape[0]
    high = field.astype(jnp.bfloat16)
    low = (field - high.astype(jnp.float32)).astype(jnp.bfloat16)
    both = jnp.dot(jnp.concatenate([high, low], axis=0), block, preferred_element_type=jnp.float32)
    return both[:rows] + both[rows:]


def ring_steps():
    return list(range(REACH + 1)) + [-distance for distance in range(1, REACH + 1)]


def front_kernel(
    tile_ref, target_hbm, delay_hbm, link_hbm, near_hbm, jacobi_hbm, voltage_hbm, history_hbm, blocks_hbm,
    bucket_ref, own_ref, kept_ref, gates_ref,
    target_ref, delay_ref, link_ref, near_ref, jacobi_ref, voltage_ref, history_ref, blocks_ref, sems, block_sems,
):
    entries, chunks = blocks_ref.shape[0], block_sems.shape[0]
    step = entries // chunks
    pairs = [
        (target_hbm, target_ref), (delay_hbm, delay_ref), (link_hbm, link_ref),
        (near_hbm, near_ref), (jacobi_hbm, jacobi_ref), (voltage_hbm, voltage_ref),
        (history_hbm, history_ref),
    ]
    copies = [pltpu.make_async_copy(a, b, sems.at[i]) for i, (a, b) in enumerate(pairs)]
    slabs = [
        pltpu.make_async_copy(
            blocks_hbm.at[pl.ds(c * step, step)], blocks_ref.at[pl.ds(c * step, step)], block_sems.at[c]
        )
        for c in range(chunks)
    ]
    for copy in copies + slabs:
        copy.start()
    bucket_ref[...] = jnp.zeros_like(bucket_ref)
    for copy in copies:
        copy.wait()
    jacobi = jacobi_ref[...]
    kept_ref[...] = jacobi
    for side in range(2):
        gates_ref[side : side + 1] = jnp.full((1, gates_ref.shape[1]), link_ref[side].astype(jnp.float32))
    for side, gate in enumerate((link_ref[0], 1, link_ref[1])):
        near = near_ref[side]
        product = jnp.dot(near, jacobi, preferred_element_type=jnp.float32)
        merged = near.astype(jnp.float32) + product
        own_ref[side] = merged + jacobi.astype(jnp.float32) if side == 1 else merged * gate.astype(jnp.float32)
    bucket_ref[tile_ref[0]] = -voltage_ref[...]
    for c in range(chunks):
        slabs[c].wait()
        for entry in range(c * step, (c + 1) * step):
            target = target_ref[entry]
            product = jnp.dot(
                history_ref[delay_ref[entry] - 1],
                blocks_ref[entry],
                preferred_element_type=jnp.float32,
            )
            bucket_ref[target] = bucket_ref[target] + product


def front_call(tile, inputs, tiles):
    near, jacobi, voltage = inputs[3:6]
    f32 = jnp.float32
    spaces = [pltpu.SMEM] * 3 + [pltpu.VMEM] * 5
    return call(
        front_kernel,
        (
            jax.ShapeDtypeStruct((tiles,) + voltage.shape, f32),
            jax.ShapeDtypeStruct(near.shape, f32),
            jax.ShapeDtypeStruct(jacobi.shape, jacobi.dtype),
            jax.ShapeDtypeStruct((2, jacobi.shape[0]), f32),
        ),
        "s" + "h" * len(inputs),
        scratch_shapes=[space(x.shape, x.dtype) for space, x in zip(spaces, inputs)]
        + [pltpu.SemaphoreType.DMA((len(inputs) - 1,)), pltpu.SemaphoreType.DMA((1,))],
    )(tile, *inputs)


def start_kernel(received_ref, jacobi_ref, out_ref):
    right_side = -jnp.sum(received_ref[...], axis=0)
    out_ref[...] = right_side + split_dot(right_side, jacobi_ref[...])


def krylov_kernel(place_ref, start_ref, *refs):
    steps = ring_steps()
    given_ref = refs[REACH + 1]
    piece_refs = list(refs[: REACH + 1]) + [given_ref.at[i] for i in range(REACH)]
    gram_ref, own_ref, fields, parts, highs, lows, sums = refs[REACH + 2 :]
    rows, scenarios, segments = start_ref.shape
    place = place_ref[0]
    core = lax.rem(place, CORES)
    middle = ITERS

    def halves(value):
        high = value.astype(jnp.bfloat16)
        low = (value - high.astype(jnp.float32)).astype(jnp.bfloat16)
        return high, low

    def inside(tile):
        return jnp.where((tile >= 0) & (tile < rows), 1.0, 0.0)

    for piece_ref, step in zip(piece_refs, steps):
        for there in range(CORES):
            away = (2 * core - 1) * (step * CORES) + there - core
            block = piece_ref[there].reshape(highs.shape[1:]) * inside(place + away)
            highs[away + middle], lows[away + middle] = halves(block)
    for away in range(-middle, middle + 1):
        tile = place + away
        field = start_ref[jnp.clip(tile, 0, rows - 1)] * inside(tile)
        parts[0, away + middle] = jnp.concatenate(halves(field), axis=0)
        if away == 0:
            fields[0] = field

    for k in range(ITERS):
        reach = ITERS - 1 - k
        for t in range(middle - reach, middle + reach + 1):
            around = jnp.concatenate([parts[k, t - 1], parts[k, t], parts[k, t + 1]], axis=1)
            main = jnp.dot(around, highs[t], preferred_element_type=jnp.float32)
            rest = jnp.dot(around[:scenarios], lows[t], preferred_element_type=jnp.float32)
            value = main[:scenarios] + (main[scenarios:] + rest)
            if t == middle:
                fields[k + 1] = value
            if k + 1 < ITERS:
                parts[k + 1, t] = jnp.concatenate(halves(value), axis=0)

    values = [fields[i] for i in range(BASIS)]
    for p, (i, j) in enumerate(PAIRS):
        sums[p] = values[i] * values[j]
    for p in range(len(PAIRS), sums.shape[0]):
        sums[p] = jnp.zeros((scenarios, segments), jnp.float32)
    total = lax.dot_general(
        jnp.ones((8, segments), jnp.float32),
        sums[...].reshape(sums.shape[0] * scenarios, segments),
        (((1,), (1,)), ((), ())),
        precision=PRECISE,
        preferred_element_type=jnp.float32,
    )
    gram_ref[...] = jnp.broadcast_to(total[0:1][None], gram_ref.shape)
    for j in range(ITERS):
        own_ref[j] = fields[j]


def krylov_call(place, starts, pieces, tiles=32):
    rows, scenarios, segments = starts.shape
    f32, bf16 = jnp.float32, jnp.bfloat16
    padded_pairs = -(-len(PAIRS) * scenarios // 128) * 128 // scenarios
    span = 2 * ITERS + 1
    return call(
        krylov_kernel,
        (
            jax.ShapeDtypeStruct((tiles, 1, padded_pairs * scenarios), f32),
            jax.ShapeDtypeStruct((ITERS, scenarios, segments), f32),
        ),
        "sv" + "v" * len(pieces),
        scratch_shapes=[
            pltpu.VMEM((BASIS, scenarios, segments), f32),
            pltpu.VMEM((ITERS, span, 2 * scenarios, segments), bf16),
            pltpu.VMEM((span, 3 * segments, segments), bf16),
            pltpu.VMEM((span, 3 * segments, segments), bf16),
            pltpu.VMEM((padded_pairs, scenarios, segments), f32),
        ],
    )(place, starts, *pieces)


def add_kernel(received_ref, out_ref):
    total = jnp.sum(received_ref[...], axis=0)
    out_ref[...] = jnp.broadcast_to(total[None], out_ref.shape)


def solve_kernel(received_ref, fields_ref, out_ref, safe_ref):
    total = jnp.sum(received_ref[...], axis=0)
    scenarios = out_ref.shape[0]
    gram = {pair: total[:, p * scenarios : (p + 1) * scenarios] for p, pair in enumerate(PAIRS)}
    factor = {}
    safe = jnp.ones((1, scenarios), jnp.float32)
    for i in range(BASIS):
        pivot = gram[i, i]
        for k in range(i):
            pivot = pivot - factor[k, i] * factor[k, i]
        safe = jnp.where(pivot >= PIVOT_SHARE * gram[i, i], safe, 0.0)
        safe = jnp.where(pivot > 0.0, safe, 0.0)
        safe = jnp.where(gram[i, i] < jnp.inf, safe, 0.0)
        factor[i, i] = jnp.sqrt(pivot)
        for j in range(i + 1, BASIS):
            entry = gram[i, j]
            for k in range(i):
                entry = entry - factor[k, i] * factor[k, j]
            factor[i, j] = entry / factor[i, i]
    matrix = [[None] * ITERS for _ in range(BASIS)]
    for j in range(ITERS):
        for i in range(j + 1):
            matrix[i][j] = factor[i, j] + factor[i, j + 1]
        matrix[j + 1][j] = factor[j + 1, j + 1]
    target = [factor[0, 0]] + [None] * ITERS
    for j in range(ITERS):
        diagonal, below = matrix[j][j], matrix[j + 1][j]
        radius = jnp.sqrt(diagonal * diagonal + below * below)
        cosine, sine = diagonal / radius, below / radius
        matrix[j][j] = radius
        for k in range(j + 1, ITERS):
            upper, lower = matrix[j][k], matrix[j + 1][k]
            matrix[j][k] = cosine * upper + sine * lower
            matrix[j + 1][k] = cosine * lower - sine * upper
        target[j + 1] = -sine * target[j]
        target[j] = cosine * target[j]
    coeffs = [None] * ITERS
    for j in reversed(range(ITERS)):
        partial = target[j]
        for k in range(j + 1, ITERS):
            partial = partial - matrix[j][k] * coeffs[k]
        coeffs[j] = partial / matrix[j][j]
    padded = jnp.concatenate(coeffs + [jnp.zeros((8 - ITERS, scenarios), jnp.float32)], axis=0)
    padded = jnp.concatenate([padded, jnp.zeros((8, 128 - scenarios), jnp.float32)], axis=1)
    columns = jnp.transpose(padded)[:scenarios]
    result = columns[:, 0:1] * fields_ref[0]
    for j in range(1, ITERS):
        result = result + columns[:, j : j + 1] * fields_ref[j]
    out_ref[...] = result
    safe_ref[0] = jnp.min(safe)


def gather_blocks(own):
    size = CHIPS * CORES
    pairs = [[CORES * chip + core for core in range(CORES)] for chip in range(CHIPS)]
    ring = [(i, (i + (CORES if i % CORES == 0 else -CORES)) % size) for i in range(size)]
    swap = [(i, i ^ 1) for i in range(size)]
    piece = lax.all_gather(own, "row", axis_index_groups=pairs)
    pieces = [piece]
    for _ in range(REACH):
        piece = lax.ppermute(piece, "row", ring)
        pieces.append(piece)
    return pieces + [lax.ppermute(jnp.stack(pieces[1:]), "row", swap)]


def neighbours(field):
    size = lax.axis_size("row")
    up = [(i, i + 1) for i in range(size - 1)]
    down = [(j, i) for i, j in up]
    return lax.ppermute(field, "row", up), lax.ppermute(field, "row", down)


def near_apply(field, near_f32, link_gain):
    lower, upper = neighbours(field)
    result = field + jnp.dot(field, near_f32[1], precision=PRECISE)
    result = result + link_gain[0] * jnp.dot(lower, near_f32[0], precision=PRECISE)
    return result + link_gain[1] * jnp.dot(upper, near_f32[2], precision=PRECISE)


def jacobi_apply(field, jacobi_f32):
    return field + jnp.dot(field, jacobi_f32, precision=PRECISE)


def givens_solve(hessen, start_norm):
    matrix = [[hessen[i][k] for k in range(ITERS)] for i in range(ITERS + 1)]
    target = [start_norm] + [jnp.zeros_like(start_norm) for k in range(ITERS)]
    for j in range(ITERS):
        diag_val = matrix[j][j]
        below_val = matrix[j + 1][j]
        radius = jnp.sqrt(diag_val * diag_val + below_val * below_val)
        cosine = diag_val / radius
        sine_val = below_val / radius
        for k in range(j, ITERS):
            upper_val = matrix[j][k]
            lower_val = matrix[j + 1][k]
            matrix[j][k] = cosine * upper_val + sine_val * lower_val
            matrix[j + 1][k] = cosine * lower_val - sine_val * upper_val
        target[j + 1] = -sine_val * target[j]
        target[j] = cosine * target[j]
    coeffs = [None] * ITERS
    for j in reversed(range(ITERS)):
        partial_val = target[j]
        for k in range(j + 1, ITERS):
            partial_val = partial_val - matrix[j][k] * coeffs[k]
        coeffs[j] = partial_val / matrix[j][j]
    return coeffs


def stepwise_solve(initial, near, jacobi, link_gain):
    near_f32 = near.astype(jnp.float32)
    jacobi_f32 = jacobi.astype(jnp.float32)
    start_norm = jnp.sqrt(lax.psum(jnp.sum(initial * initial, axis=1), ("tile", "row")))
    basis = [initial / start_norm[:, None]]
    zero_row = jnp.zeros_like(start_norm)
    hessen = [[zero_row for k in range(ITERS)] for i in range(ITERS + 1)]
    for j in range(ITERS):
        candidate = jacobi_apply(near_apply(basis[j], near_f32, link_gain), jacobi_f32)
        local_dots = jnp.stack([jnp.sum(v * candidate, axis=1) for v in basis])
        projections = lax.psum(local_dots, ("tile", "row"))
        for i in range(j + 1):
            candidate = candidate - projections[i][:, None] * basis[i]
        new_norm = jnp.sqrt(lax.psum(jnp.sum(candidate * candidate, axis=1), ("tile", "row")))
        for i in range(j + 1):
            hessen[i][j] = projections[i]
        hessen[j + 1][j] = new_norm
        basis.append(candidate / new_norm[:, None])
    coeffs = givens_solve(hessen, start_norm)
    result = coeffs[0][:, None] * basis[0]
    for j in range(1, ITERS):
        result = result + coeffs[j][:, None] * basis[j]
    return result


def per_device(
    voltage, history, far_blocks, far_target, far_delay, near_blocks, near_link, jacobi_blocks
):
    voltage = voltage[0, 0, 0]
    history = history[0, 0]
    far_blocks = far_blocks[0, 0]
    targets = far_target[0, 0, :, 0]
    delays = far_delay[0, 0]
    near = near_blocks[0, 0]
    link = near_link[0, 0]
    jacobi = jacobi_blocks[0, 0]
    tiles, rows = lax.axis_size("tile"), lax.axis_size("row")
    scenarios, segments = voltage.shape
    f32 = jnp.float32
    field_shape = jax.ShapeDtypeStruct((scenarios, segments), f32)

    tile = lax.axis_index("tile").astype(jnp.int32)[None]
    bucket, own_blocks, jacobi_kept, gates = front_call(
        tile, (targets, delays, link, near, jacobi, voltage, history, far_blocks), tiles
    )
    received = lax.all_to_all(bucket, "tile", split_axis=0, concat_axis=0, tiled=True)
    pieces = gather_blocks(own_blocks)
    initial = call(start_kernel, field_shape, "vv")(received, jacobi_kept)
    starts = lax.all_gather(initial, "row")
    place = lax.axis_index("row").astype(jnp.int32)[None]
    gram, own = krylov_call(place, starts, pieces, tiles)
    by_tile = lax.all_to_all(gram, "tile", split_axis=0, concat_axis=0, tiled=True)
    group = call(add_kernel, jax.ShapeDtypeStruct((rows,) + gram.shape[1:], f32), "v")(by_tile)
    by_row = lax.all_to_all(group, "row", split_axis=0, concat_axis=0, tiled=True)
    result, safe = call(
        solve_kernel,
        (field_shape, jax.ShapeDtypeStruct((1,), f32)),
        "vv",
        out_specs=(pl.BlockSpec(memory_space=pltpu.VMEM), pl.BlockSpec(memory_space=pltpu.SMEM)),
    )(by_row, own)
    safe, result = lax.while_loop(
        lambda state: state[0][0] < 0.5,
        lambda state: (jnp.ones_like(state[0]), stepwise_solve(initial, near, jacobi_kept, gates)),
        (safe, result),
    )
    return result[None, None, None]


def solution(mesh):
    return jax.shard_map(
        per_device,
        mesh=mesh,
        in_specs=(
            P("tile", "row", None, None, None),
            P("tile", "row", None, None, None),
            P("tile", "row", None, None, None),
            P("tile", "row", None, None),
            P("tile", "row", None),
            P("tile", "row", None, None, None),
            P("tile", "row", None),
            P("tile", "row", None, None),
        ),
        out_specs=P("tile", "row", None, None, None),
        check_vma=False,
    )
```
